32 devices in a mesh: vec: 8 (over z, core), rep: 4 (over y, x).
Axes of the slice: x: 2, y: 2, z: 4, core: 2. Of those that a mesh axis runs over, the one named last changes fastest.
Arguments:
- vectors: bfloat16 [1024, 1024], P('vec'), may hold values from 0 to 2
- pivot_index: int32 [4, 8], P('rep'), may hold values from 0 to 1023
Outputs:
- similarity: bfloat16 [7, 32, 1024, 128], P(None, 'rep', 'vec')
The draws below stay inside these ranges and needn't reach their ends.
All inputs are finite; a program needn't handle non-finite values.
Results may differ from the reference program's by a relative error of at most 0.011.
Values may be sent and summed in bfloat16 or wider, within the bound.
A program may use at most 64 MiB of HBM per device.

```python
import math
import jax
import jax.numpy as jnp
from jax import lax

F = 1024
VB = 128
PIV = 8
HALF = 3
WIN = 7
NV = 1024
PIVOTS = 32
N_VEC = 8
N_REP = 4


def plant(array, rng, least, high):
    longest = array.shape.index(max(array.shape))
    spots = []
    for shift in (0, 1):
        where = [jax.random.randint(jax.random.fold_in(rng, axis), (), 0, length) for axis, length in enumerate(array.shape)]
        where[longest] = (where[longest] + shift) % array.shape[longest]
        spots.append(tuple(where))
    return array.at[spots[0]].set(least).at[spots[1]].set(high)


def steps_of(rng, dims, cuts, least, high):
    loudness = 1.0
    for dim, shards_of in cuts:
        steps = jax.random.uniform(jax.random.fold_in(jax.random.fold_in(rng, 6), dim), (shards_of,), jnp.float32, least / len(cuts), high / len(cuts))
        loudness = loudness * jnp.repeat(jnp.exp(steps), dims[dim] // shards_of).reshape((-1,) + (1,) * (len(dims) - 1 - dim))
    return loudness


def setup_inputs(seed: int = 0) -> dict:
    key_of = jax.random.split(jax.random.key(seed), 3)
    return {
        "vectors": jnp.clip(2.0 * jax.random.uniform(key_of[0], (NV, F), jnp.float32) ** steps_of(key_of[0], (NV, F), ((0, 8),), -0.2, 0.2), 0.0, 2.0).astype(jnp.bfloat16),
        "pivot_index": plant(jax.random.randint(key_of[1], (N_REP, PIV), 0, NV), jax.random.fold_in(key_of[1], 1), 0, NV - 1).astype(jnp.int32),
    }


def reference(vectors, pivot_index):
    chosen = pivot_index.reshape(-1).astype(jnp.int32)
    pivots = vectors[chosen]
    centre = lax.optimization_barrier(jnp.sum(pivots.astype(jnp.float32), axis=1)) / F
    blocks = vectors.reshape(N_VEC, VB, F).astype(jnp.float32)
    pair_gram = jnp.stack([jnp.einsum('iaf,ibf->iab', blocks, jnp.roll(blocks, HALF - offset, axis=0), precision=lax.Precision.HIGHEST) for offset in range(WIN)])

    def one_pivot(inputs):
        pivot_row, level = inputs
        scaled = (vectors.astype(jnp.float32) * pivot_row.astype(jnp.float32)[None, :]).astype(jnp.bfloat16)
        scaled = lax.optimization_barrier(scaled)
        scaled_blocks = scaled.reshape(N_VEC, VB, F).astype(jnp.float32)
        pieces = []
        for offset in range(WIN):
            triple = jnp.einsum('iaf,ibf->iab', scaled_blocks, jnp.roll(blocks, HALF - offset, axis=0), precision=lax.Precision.HIGHEST)
            pieces.append(((triple - level * pair_gram[offset]) / math.sqrt(F)).astype(jnp.bfloat16))
        return jnp.stack(pieces)
    result = lax.map(one_pivot, (pivots, centre))
    return result.reshape(PIVOTS, WIN, NV, VB).transpose(1, 0, 2, 3)
```

```python
import functools
import math

import jax
import jax.numpy as jnp
from jax import lax
from jax.experimental import pallas as pl
from jax.experimental.pallas import tpu as pltpu
from jax.sharding import PartitionSpec as P

HALF = 3
NEAR, OUTER, FAR = 0, 1, 2


def contract(left, right):
    return lax.dot_general(
        left, right, (((1,), (1,)), ((), ())), preferred_element_type=jnp.float32
    )


def inward(chip, chips):
    return 1 - 2 * (2 * chip // chips) if chips <= 4 else 1 + 0 * chip


def place(slot, core, way):
    if slot == FAR:
        return 2 * HALF * core
    step = way if slot == NEAR else -way
    return HALF + 2 * step, HALF + 2 * step + 1 - 2 * core


def products(scaled, right, count):
    fields = scaled.shape[1]
    value = (contract(scaled, right) * (1.0 / math.sqrt(fields))).astype(jnp.bfloat16)
    return value.reshape(count, scaled.shape[0] // count, right.shape[0])


def closing(n_vec, held, win, scaled, out_ref, last, sems):
    window, count, block_rows, _ = held.shape
    core = lax.axis_index("vec") % 2
    spot = place(FAR, core, 1)

    def ready(i):
        return pltpu.make_async_copy(held.at[i], out_ref.at[i], sems.at[i])

    late = pltpu.make_async_copy(last, out_ref.at[spot], sems.at[window])
    for i in range(window):
        pl.when(spot != i)(lambda i=i: ready(i).start())
    last[...] = products(scaled[...], win[6], count)
    late.start()
    for i in range(window):
        pl.when(spot != i)(lambda i=i: ready(i).wait())
    late.wait()


def kernel(
    n_vec, n_a, n_b, vec_ref, index_ref, out_ref, win, scaled, wanted_ref, rows_ref, heard,
    z_send, z_recv, f_send, f_recv, d_send, d_recv, r_send, r_recv, p_send, p_recv,
    h_send, h_recv, o_send, o_recv, local_sem, allow,
):
    block_rows, fields = vec_ref.shape
    count = index_ref.shape[1]
    n_rep = n_a * n_b
    chips = n_vec // 2
    part = block_rows // n_rep
    piece = part // 2
    me = lax.axis_index("vec")
    rep = lax.axis_index("rep")
    a, b = rep // n_b, rep % n_b
    chip, core = me // 2, me % 2
    partner = {"vec": me + 1 - 2 * core}
    way = inward(chip, chips)
    short = n_vec <= 16

    def at_chip(offset, which):
        return {"vec": 2 * ((chip + offset + chips) % chips) + which}

    def rep_of(da, db):
        return ((a + da + n_a) % n_a) * n_b + (b + db + n_b) % n_b

    direct = [(0, i) for i in range(1, n_b)] + [(i, 0) for i in range(1, n_a)]
    diagonal = [(i, j) for i in range(1, n_a) for j in range(1, n_b)]
    relays = {}
    for t, (da, db) in enumerate(direct):
        if da == 0:
            relays[t] = [((i, 0), diagonal.index((i, db))) for i in range(1, n_a)]
        else:
            relays[t] = [((0, j), diagonal.index((da, j))) for j in range(1, n_b)]
    side = [0 if da == 0 else 1 for da, _ in direct]

    own_copy = pltpu.make_async_copy(vec_ref, win.at[0], local_sem.at[0])
    index_copy = pltpu.make_async_copy(index_ref, wanted_ref, local_sem.at[1])
    own_copy.start()
    index_copy.start()

    def chip_index(offset):
        return (chip + offset + chips) % chips

    def is_up(offset):
        return chip_index(offset) > chip

    def rep_is_up(da, db):
        return rep_of(da, db) > rep

    def number_of(flags):
        return sum(flag.astype(jnp.int32) for flag in flags)

    def everywhere(action):
        def body(i, carry):
            action(i)
            return carry

        lax.fori_loop(1, chips, body, 0, unroll=short)

    barrier = pltpu.get_barrier_semaphore()

    def meet(sem, when, device):
        pl.when(when)(lambda: pl.semaphore_signal(sem, inc=1, device_id=device))

    sides = (1, -1)
    everywhere(lambda i: meet(barrier, is_up(i), at_chip(i, core)))
    for step in sides:
        meet(barrier, is_up(step), at_chip(step, 1 - core))
    for hop in direct:
        meet(barrier, rep_is_up(*hop), {"rep": rep_of(*hop)})
    pl.semaphore_signal(barrier, inc=1, device_id=partner)
    ups = number_of([is_up(step) for step in sides])
    rep_ups = number_of([rep_is_up(*hop) for hop in direct]) if direct else jnp.int32(0)
    pl.semaphore_wait(barrier, chip + (2 - ups) + (len(direct) - rep_ups) + 1)
    meet(allow.at[0], jnp.logical_not(is_up(-1)), at_chip(-1, core))
    everywhere(lambda i: meet(allow.at[1], jnp.logical_not(is_up(i)), at_chip(i, core)))
    for hop in direct:
        meet(allow.at[2], jnp.logical_not(rep_is_up(*hop)), {"rep": rep_of(*hop)})
    for step in sides:
        meet(allow.at[3], jnp.logical_not(is_up(step)), at_chip(step, 1 - core))

    def allowed(i, times):
        pl.when(times > 0)(lambda: pl.semaphore_wait(allow.at[i], times))

    def remote(src, dst, send_sem, recv_sem, device):
        return pltpu.make_async_remote_copy(
            src_ref=src, dst_ref=dst, send_sem=send_sem, recv_sem=recv_sem, device_id=device
        )

    sent = []

    def start(make, *args):
        make(*args).start()
        sent.append((make, args))

    def rows_at(which, h):
        return pl.ds(pl.multiple_of(which * part + h * piece, piece), piece)

    def quarter(da, db, h):
        return rows_at(rep_of(-da, -db), h)

    own = [rows_at(rep, h) for h in range(2)]

    def z_copy(step, h):
        target = (chip + step + chips) % chips
        slot = (1 - step * inward(target, chips) * -1) // 2
        return remote(
            vec_ref.at[own[h]], win.at[2 + 2 * slot, own[h]], z_send.at[(1 - step) // 2, h],
            z_recv.at[slot, h], at_chip(step, core),
        )

    def z_arrival(slot, h):
        spot = win.at[2 + 2 * slot, own[h]]
        return remote(spot, spot, z_send.at[0, 0], z_recv.at[slot, h], partner)

    def rows_out(i):
        return remote(rows_ref, heard.at[i], p_send.at[i], p_recv.at[i], at_chip(i, core))

    rows_partner = remote(rows_ref, heard.at[0], p_send.at[0], p_recv.at[0], partner)

    def rows_across(i):
        k = chips - 1 + i
        return remote(heard.at[i], heard.at[k], p_send.at[k], p_recv.at[k], partner)

    def passes(slot):
        if chips <= 4:
            return jnp.logical_and(chip != 0, chip != chips - 1)
        return core == slot

    def pass_on(slot, h):
        step = -way if slot == NEAR else way
        return remote(
            win.at[2 + 2 * slot, own[h]], win.at[6, own[h]], f_send.at[slot, h], f_recv.at[h],
            at_chip(step, 1 - core),
        )

    def far_arrival(h):
        spot = win.at[6, own[h]]
        return remote(spot, spot, f_send.at[0, 0], f_recv.at[h], partner)

    def d_copy(slot, t, h):
        spot = win.at[2 + 2 * slot, own[h]]
        return remote(spot, spot, d_send.at[slot, t, h], d_recv.at[slot, t, h], {"rep": rep_of(*direct[t])})

    def r_copy(slot, t, hop, number):
        spot = win.at[2 + 2 * slot, quarter(*direct[t], side[t])]
        k = 2 * number + side[t]
        return remote(spot, spot, r_send.at[slot, k], r_recv.at[slot, k], {"rep": rep_of(*hop)})

    hands = [0, 0]

    def hand(slot, rows):
        if slot == FAR:
            return
        k = hands[slot]
        hands[slot] += 1
        start(lambda: remote(
            win.at[2 + 2 * slot, rows()], win.at[3 + 2 * slot, rows()], h_send.at[slot, k],
            h_recv.at[slot], partner,
        ))

    def handed(slot):
        spot = win.at[3 + 2 * slot]
        remote(spot, spot, h_send.at[slot, 0], h_recv.at[slot], partner).wait_recv()

    def first(slot, h):
        (far_arrival(h) if slot == FAR else z_arrival(slot, h)).wait_recv()
        for t in range(len(direct)):
            start(d_copy, slot, t, h)
        hand(slot, lambda: own[h])

    def second(slot, h):
        for t in range(len(direct)):
            d_copy(slot, t, h).wait_recv()
            if side[t] == h:
                for hop, number in relays[t]:
                    start(r_copy, slot, t, hop, number)
            hand(slot, lambda t=t: quarter(*direct[t], h))

    def third(slot):
        for number in range(len(diagonal)):
            for h in range(2):
                spot = win.at[2 + 2 * slot, quarter(*diagonal[number], h)]
                k = 2 * number + h
                remote(spot, spot, r_send.at[slot, k], r_recv.at[slot, k], partner).wait_recv()
                hand(slot, lambda number=number, h=h: quarter(*diagonal[number], h))

    partner_own = remote(vec_ref, win.at[1], o_send.at[0], o_recv.at[0], partner)

    def scope(name, action, *args):
        with jax.named_scope(name):
            return action(*args)

    def prepare():
        pivots = lax.fori_loop(
            0, n_vec - 1, lambda i, total: total + heard[i].astype(jnp.float32),
            rows_ref[...].astype(jnp.float32), unroll=short,
        )
        level = jnp.sum(pivots, axis=1, keepdims=True) / fields
        pivots = pivots - level
        block = win[0].astype(jnp.float32)
        for k in range(count):
            scaled[k * block_rows:(k + 1) * block_rows, :] = (block * pivots[k:k + 1, :]).astype(jnp.bfloat16)

    def compare(i):
        step = way * (i % 2) - way * (i // 2)
        mine_at = HALF + 2 * step
        other_at = mine_at + 1 - 2 * core
        value = products(scaled[...], win[pl.ds(2 * i, 2)].reshape(2 * block_rows, fields), count)
        out_ref[mine_at] = value[:, :, :block_rows]
        out_ref[other_at] = value[:, :, block_rows:]

    lower = jnp.logical_not
    for h in range(2):
        for step in (-1, 1):
            pl.when(lower(is_up(step)))(lambda: z_copy(step, h).start())
    partner_own.start()

    index_copy.wait()
    own_copy.wait()
    wanted = wanted_ref[...] - me * block_rows
    spots = lax.broadcasted_iota(jnp.int32, (block_rows, count), 0)
    onehot = (spots == wanted).astype(jnp.bfloat16)
    mine = lax.dot_general(
        onehot, win[0], (((0,), (0,)), ((), ())), preferred_element_type=jnp.float32
    )
    rows_ref[...] = mine.astype(jnp.bfloat16)
    rows_partner.start()
    everywhere(lambda i: pl.when(lower(is_up(i)))(lambda: rows_out(i).start()))

    @pl.when(is_up(1))
    def _():
        pl.semaphore_wait(allow.at[0], 1)
        for h in range(2):
            z_copy(1, h).start()

    def pass_rows(i):
        rows_out(i).wait_recv()
        rows_across(i).start()

    allowed(2, rep_ups)
    scope("z00", first, NEAR, 0)
    scope("z01", first, NEAR, 1)
    allowed(3, ups)
    allowed(1, chips - 1 - chip)
    for h in range(2):
        pl.when(is_up(-1))(lambda: z_copy(-1, h).start())
    everywhere(lambda i: pl.when(is_up(i))(lambda: rows_out(i).start()))
    for h in range(2):
        pl.when(passes(NEAR))(lambda: pass_on(NEAR, h).start())
    scope("z10", first, OUTER, 0)
    scope("z11", first, OUTER, 1)
    for h in range(2):
        pl.when(passes(OUTER))(lambda: pass_on(OUTER, h).start())
    scope("d00", second, NEAR, 0)
    scope("d01", second, NEAR, 1)
    scope("z20", first, FAR, 0)
    scope("z21", first, FAR, 1)
    scope("passrows", everywhere, pass_rows)
    scope("d10", second, OUTER, 0)
    scope("d11", second, OUTER, 1)
    scope("r0", third, NEAR)
    scope("d20", second, FAR, 0)
    scope("d21", second, FAR, 1)
    scope("rp", rows_partner.wait_recv)
    scope("ra", everywhere, lambda i: rows_across(i).wait_recv())
    scope("scaled", prepare)
    scope("po", partner_own.wait_recv)

    def body(i, carry):
        @pl.when(i == 1)
        def _():
            scope("r1", third, OUTER)
            scope("h0", handed, NEAR)

        pl.when(i == 2)(lambda: scope("h1", handed, OUTER))
        scope("cmp", compare, i)
        return carry

    lax.fori_loop(0, 3, body, 0)
    scope("r2", third, FAR)
    with jax.named_scope("drain"):
        for make, args in sent:
            make(*args).wait_send()
        for h in range(2):
            for step in sides:
                z_copy(step, h).wait_send()
        for slot in (NEAR, OUTER):
            for h in range(2):
                pl.when(passes(slot))(lambda: pass_on(slot, h).wait_send())
        rows_partner.wait_send()
        partner_own.wait_send()
        everywhere(lambda i: rows_out(i).wait_send())
        everywhere(lambda i: rows_across(i).wait_send())


def solution(mesh):
    n_vec, n_rep = mesh.shape["vec"], mesh.shape["rep"]
    n_b = 2 if n_rep % 2 == 0 else 1
    n_a = n_rep // n_b
    assert n_vec % 2 == 0 and n_vec > 2 * HALF

    def step(vectors, pivot_index):
        rows, fields = vectors.shape
        count = pivot_index.shape[1]
        direct = max(n_a + n_b - 2, 1)
        diagonal = max((n_a - 1) * (n_b - 1), 1)
        dma = pltpu.SemaphoreType.DMA
        vmem = pl.BlockSpec(memory_space=pltpu.VMEM)
        hbm = pl.BlockSpec(memory_space=pltpu.HBM)
        held, win, scaled = pl.pallas_call(
            functools.partial(kernel, n_vec, n_a, n_b),
            out_shape=(
                pltpu.VMEM((2 * HALF + 1, count, rows, rows), jnp.bfloat16),
                pltpu.VMEM((7, rows, fields), jnp.bfloat16),
                pltpu.VMEM((count * rows, fields), jnp.bfloat16),
            ),
            in_specs=[hbm, hbm],
            out_specs=(vmem, vmem, vmem),
            scratch_shapes=[
                pltpu.VMEM((1, count), jnp.int32),
                pltpu.VMEM((count, fields), jnp.bfloat16),
                pltpu.VMEM((n_vec - 1, count, fields), jnp.bfloat16),
                dma((2, 2)), dma((2, 2)),
                dma((2, 2)), dma((2,)),
                dma((3, direct, 2)), dma((3, direct, 2)),
                dma((3, 2 * diagonal)), dma((3, 2 * diagonal)),
                dma((n_vec - 1,)), dma((n_vec - 1,)),
                dma((2, 2 * (1 + direct + diagonal))), dma((2,)),
                dma((1,)), dma((1,)),
                dma((2,)), pltpu.SemaphoreType.REGULAR((4,)),
            ],
            compiler_params=pltpu.CompilerParams(
                collective_id=0, has_side_effects=True, vmem_limit_bytes=60_800_000
            ),
        )(vectors, pivot_index)
        return pl.pallas_call(
            functools.partial(closing, n_vec),
            out_shape=jax.ShapeDtypeStruct(held.shape, held.dtype),
            in_specs=[vmem, vmem, vmem],
            out_specs=pl.BlockSpec(memory_space=pl.ANY),
            scratch_shapes=[pltpu.VMEM(held.shape[1:], held.dtype), dma((2 * HALF + 2,))],
            compiler_params=pltpu.CompilerParams(vmem_limit_bytes=24 * 2**20),
        )(held, win, scaled)

    return jax.shard_map(
        step, mesh=mesh, in_specs=(P("vec", None), P("rep", None)),
        out_specs=P(None, "rep", "vec", None), check_vma=False,
    )
```

```python
import functools
import math

import jax
import jax.numpy as jnp
from jax import lax
from jax.experimental import pallas as pl
from jax.experimental.pallas import tpu as pltpu
from jax.sharding import PartitionSpec as P

HALF = 3
NEAR, OUTER, FAR = 0, 1, 2
AT = (3, 5, 2)
LAST = FAR
RELAY, ROUTED, WIDE = range(3)
EDGE, AMID, RING, HEAD = range(4)
def words(*parts):
    return " ".join(parts)


MODES = ((RELAY, WIDE, ROUTED), (RELAY, WIDE, RELAY), (RELAY, RELAY, RELAY))
STEPS = {
    HEAD: (words("z00 z01 up outward", "inward z10 d00 d01", "z11 z20 z21 rows"), words("r0 d10 d11 r1", "h0"), words("d20 d21 h1"), words("r2")),
    EDGE: (words("z00 z01 up outward", "inward z10 d00 d01", "z11 z20 z21 rows"), words("r0 d10 d11 d20", "d21 r1 h0"), words("h1"), words("r2")),
    AMID: (words("z00 z10 z11 z01", "up outward d00 d01", "z20 z21 r1 d10", "d11 rows"), words("h1 r0 d20 d21"), words("h0"), words("r2")),
    RING: (words("z00 z10 z01 z11", "up d00 d01 rows", "z20 z21 d10 d11", "r0 d20 d21 r1"), words("h0"), words("h1"), words("r2")),
}
CHUNKS = 1
SWAP = True


def contract(left, right):
    return lax.dot_general(
        left, right, (((1,), (1,)), ((), ())), preferred_element_type=jnp.float32
    )


def inward(chip, chips):
    return 1 - 2 * (2 * chip // chips) if chips <= 4 else 1 + 0 * chip


def pairs(i, core, way):
    if isinstance(i, int) and i == 3 and LAST == FAR:
        return 1, HALF + 1 - 2 * core, 2 * HALF * core
    if isinstance(i, int) and i == 3:
        return 5, HALF - 2 * way, HALF - 2 * way + 1 - 2 * core
    if LAST == FAR:
        step = way * (i % 2) - way * (i // 2)
        mine = HALF + 2 * step
        return (i > 0) + 2 * i, mine, mine + 1 - 2 * core
    near, far = i % 2, i // 2
    mine = HALF + 2 * way * near + far * (1 - 2 * core)
    other = (HALF + 2 * way * near + 1 - 2 * core) * (1 - far) + 2 * HALF * core * far
    return 3 * near + far, mine, other


def products(scaled, right, count):
    value = (contract(scaled, right) * (1.0 / math.sqrt(scaled.shape[1]))).astype(jnp.bfloat16)
    return value.reshape(count, scaled.shape[0] // count, right.shape[0])


def closing(n_vec, held, win, scaled, out_ref, last, sems):
    window, count, block_rows, fields = held.shape[0], held.shape[1], held.shape[2], win.shape[2]
    me = lax.axis_index("vec")
    base, first, second = pairs(3, me % 2, inward(me // 2, n_vec // 2))
    fresh = [second] if LAST == FAR else [first, second]

    def ready(i):
        return pltpu.make_async_copy(held.at[i], out_ref.at[i], sems.at[i, 0])

    some = count // CHUNKS

    def late(j, n):
        ks = pl.ds(n * some, some)
        return pltpu.make_async_copy(last.at[j, ks], out_ref.at[fresh[j], ks], sems.at[window + j, n])

    def others(action):
        for i in range(window):
            unlike = fresh[0] != i
            for spot in fresh[1:]:
                unlike = jnp.logical_and(unlike, spot != i)
            pl.when(unlike)(lambda i=i: action(i))

    with jax.named_scope("s"):
        others(lambda i: ready(i).start())
    right = win[base:base + 2].reshape(2 * block_rows, fields)
    for n in range(CHUNKS):
        with jax.named_scope(f"c{n}"):
            value = products(scaled[n * some * block_rows:(n + 1) * some * block_rows], right, some)
            for j in range(len(fresh)):
                h = 2 - len(fresh) + j
                last[j, n * some:(n + 1) * some] = value[:, :, h * block_rows:(h + 1) * block_rows]
                late(j, n).start()
    with jax.named_scope("w0"):
        others(lambda i: ready(i).wait())
    with jax.named_scope("w1"):
        for j in range(len(fresh)):
            for n in range(CHUNKS):
                late(j, n).wait()


def kernel(
    n_vec, n_a, n_b, vec_ref, index_ref, out_ref, win, scaled, wanted_ref, rows_ref, chip_ref, heard,
    out_sem, z_recv, f_recv, d_recv, r_recv, p_recv, h_recv, o_recv, local_sem, allow,
):
    block_rows, fields = vec_ref.shape
    count = index_ref.shape[1]
    n_rep = n_a * n_b
    chips = n_vec // 2
    part = block_rows // n_rep
    piece = part // 2
    me = lax.axis_index("vec")
    rep = lax.axis_index("rep")
    a, b = rep // n_b, rep % n_b
    chip, core = me // 2, me % 2
    partner = {"vec": me + 1 - 2 * core}
    way = inward(chip, chips)
    short = n_vec <= 16

    def chip_index(offset):
        return (chip + offset + chips) % chips

    def at_chip(offset, which):
        return {"vec": 2 * chip_index(offset) + which}

    def rep_of(da, db):
        return ((a + da + n_a) % n_a) * n_b + (b + db + n_b) % n_b

    direct = [(0, i) for i in range(1, n_b)] + [(i, 0) for i in range(1, n_a)]
    diagonal = [(i, j) for i in range(1, n_a) for j in range(1, n_b)]
    relays = {}
    for t, (da, db) in enumerate(direct):
        if da == 0:
            relays[t] = [((i, 0), diagonal.index((i, db))) for i in range(1, n_a)]
        else:
            relays[t] = [((0, j), diagonal.index((da, j))) for j in range(1, n_b)]
    side = [0 if da == 0 else 1 for da, _ in direct]

    own_copy = pltpu.make_async_copy(vec_ref, win.at[0], local_sem.at[0])
    index_copy = pltpu.make_async_copy(index_ref, wanted_ref, local_sem.at[1])
    own_copy.start()
    index_copy.start()

    def is_up(offset):
        return chip_index(offset) > chip

    def rep_is_up(da, db):
        return rep_of(da, db) > rep

    def number_of(flags):
        return sum((flag.astype(jnp.int32) for flag in flags), jnp.int32(0))

    def everywhere(action):
        def body(i, carry):
            action(i)
            return carry

        lax.fori_loop(1, chips, body, 0, unroll=short)

    barrier = pltpu.get_barrier_semaphore()
    lower = jnp.logical_not

    def meet(sem, when, device):
        pl.when(when)(lambda: pl.semaphore_signal(sem, inc=1, device_id=device))

    def allowed(i, times):
        pl.when(times > 0)(lambda: pl.semaphore_wait(allow.at[i], times))

    sides = (1, -1)
    everywhere(lambda i: meet(barrier, is_up(i), at_chip(i, core)))
    for step in sides:
        meet(barrier, is_up(step), at_chip(step, 1 - core))
    for hop in direct:
        meet(barrier, rep_is_up(*hop), {"rep": rep_of(*hop)})
    pl.semaphore_signal(barrier, inc=1, device_id=partner)
    ups = number_of([is_up(step) for step in sides])
    rep_ups = number_of([rep_is_up(*hop) for hop in direct])
    with jax.named_scope("barrier"):
        pl.semaphore_wait(barrier, chip + (2 - ups) + (len(direct) - rep_ups) + 1)
    meet(allow.at[0], lower(is_up(-1)), at_chip(-1, core))
    everywhere(lambda i: meet(allow.at[1], lower(is_up(i)), at_chip(i, core)))
    for hop in direct:
        meet(allow.at[2], lower(rep_is_up(*hop)), {"rep": rep_of(*hop)})
    for step in sides:
        meet(allow.at[3], lower(is_up(step)), at_chip(step, 1 - core))

    def remote(src, dst, send_sem, recv_sem, device):
        return pltpu.make_async_remote_copy(
            src_ref=src, dst_ref=dst, send_sem=send_sem, recv_sem=recv_sem, device_id=device
        )

    def arrive(rows, sem):
        spot = scaled.at[pl.ds(0, rows)]
        remote(spot, spot, out_sem.at[0], sem, partner).wait_recv()

    def gone(rows):
        spot = scaled.at[pl.ds(0, rows)]
        remote(spot, spot, out_sem.at[0], o_recv.at[0], partner).wait_send()

    def rows_at(which, h):
        return pl.ds(pl.multiple_of(which * part + h * piece, piece), piece)

    def quarter(da, db, h):
        return rows_at(rep_of(-da, -db), h)

    own = [rows_at(rep, h) for h in range(2)]

    if chips <= 4:
        edge = jnp.logical_or(chip == 0, chip == chips - 1)
    else:
        edge = chip < 0

    def z_copy(step, which):
        looks = inward(chip_index(step), chips)
        slot = (1 + step * looks) // 2
        if which < 2:
            rows = own[which]
        else:
            rows = pl.ds(pl.multiple_of(rep_of(*diagonal[which - 2]) * part, part), part)
        return remote(
            vec_ref.at[rows], win.at[AT[NEAR] + (AT[OUTER] - AT[NEAR]) * slot, rows],
            out_sem.at[0], z_recv.at[slot, jnp.minimum(which, 2)], at_chip(step, core),
        )

    def passes(slot):
        return lower(edge) if chips <= 4 else core == slot

    def pass_on(slot, h):
        step = -way if slot == NEAR else way
        return remote(
            win.at[AT[slot], own[h]], win.at[AT[FAR], own[h]], out_sem.at[0], f_recv.at[h],
            at_chip(step, 1 - core),
        )

    def d_copy(slot, t, h):
        spot = win.at[AT[slot], own[h]]
        return remote(spot, spot, out_sem.at[0], d_recv.at[slot, h], {"rep": rep_of(*direct[t])})

    def routed_copy(slot, number):
        spot = win.at[AT[slot], pl.ds(pl.multiple_of(rep * part, part), part)]
        return remote(spot, spot, out_sem.at[0], r_recv.at[slot], {"rep": rep_of(*diagonal[number])})

    def r_copy(slot, t, hop):
        spot = win.at[AT[slot], quarter(*direct[t], side[t])]
        return remote(spot, spot, out_sem.at[0], r_recv.at[slot], {"rep": rep_of(*hop)})

    def hand(slot, rows):
        if slot != FAR:
            remote(
                win.at[AT[slot], rows], win.at[AT[slot] + 1, rows], out_sem.at[0], h_recv.at[slot], partner
            ).start()

    def handed(slot):
        arrive(block_rows, h_recv.at[slot])

    half = fields // 2

    def halves(src, dst, k, device):
        return remote(src, heard.at[dst], out_sem.at[1], p_recv.at[k], device)

    give_half = halves(rows_ref.at[1 - core], 0, 0, partner)
    swap = halves(chip_ref.at[1], chips, 2, partner)

    def rows_out(i):
        return halves(chip_ref.at[0], i, 1, at_chip(i, core))

    def first(slot, h, mode):
        arrive(piece, f_recv.at[h] if slot == FAR else z_recv.at[slot, h])
        if slot != FAR:
            pl.when(passes(slot))(lambda: pass_on(slot, h).start())
        for t in range(len(direct)):
            d_copy(slot, t, h).start()
        if mode == ROUTED and h == 1:
            for number in range(len(diagonal)):
                routed_copy(slot, number).start()
        hand(slot, own[h])

    def second(slot, h, mode):
        if direct:
            arrive(len(direct) * piece, d_recv.at[slot, h])
        for t in range(len(direct)):
            if side[t] == h and mode == RELAY:
                for hop, number in relays[t]:
                    r_copy(slot, t, hop).start()
            hand(slot, quarter(*direct[t], h))

    def third(slot, mode):
        if diagonal:
            arrive(len(diagonal) * part, z_recv.at[slot, 2] if mode == WIDE else r_recv.at[slot])
        for spot in diagonal:
            for h in range(2):
                hand(slot, quarter(*spot, h))

    partner_own = remote(vec_ref, win.at[1], out_sem.at[0], o_recv.at[0], partner)

    def prepare():
        mine, other = chip_ref[1].astype(jnp.float32), heard[chips].astype(jnp.float32)
        pivots = jnp.concatenate(
            [jnp.where(core == 0, mine, other), jnp.where(core == 0, other, mine)], axis=1
        )
        level = jnp.sum(pivots, axis=1, keepdims=True) / fields
        pivots = pivots - level
        block = win[0].astype(jnp.float32)
        for k in range(count):
            scaled[k * block_rows:(k + 1) * block_rows, :] = (block * pivots[k:k + 1, :]).astype(jnp.bfloat16)

    def compare(i):
        base, mine_at, other_at = pairs(i, core, way)
        value = products(scaled[...], win[pl.ds(base, 2)].reshape(2 * block_rows, fields), count)
        out_ref[mine_at] = value[:, :, :block_rows]
        out_ref[other_at] = value[:, :, block_rows:]

    def send_z(step, steps):
        for which in steps:
            z_copy(step, which).start()

    def send_wide(step):
        if diagonal:
            send_z(step, range(2, 2 + len(diagonal)))

    def extra(role):
        if role == EDGE:
            return MODES[AMID][OUTER] == WIDE, MODES[EDGE][OUTER] == WIDE
        return MODES[AMID][NEAR] == WIDE, MODES[EDGE][NEAR] == WIDE

    def up():
        allowed(1, chips - 1 - chip)
        pl.when(is_up(-1))(lambda: send_z(-1, range(2)))
        everywhere(lambda i: pl.when(is_up(i))(lambda: rows_out(i).start()))

    def add_rows():
        spot = heard.at[pl.ds(1, chips - 1)]
        remote(spot, spot, out_sem.at[1], p_recv.at[1], partner).wait_recv()
        total = lax.fori_loop(
            1, chips, lambda i, total: total + heard[i].astype(jnp.float32),
            chip_ref[0].astype(jnp.float32), unroll=short,
        )
        chip_ref[1] = total.astype(jnp.bfloat16)
        swap.start()

    def run(steps, role):
        for name in steps.split():
            slot = int(name[1]) if name[1].isdigit() else None
            with jax.named_scope(name):
                if name == "up":
                    up()
                elif name in ("inward", "outward"):
                    if extra(role)[name == "outward"]:
                        for step in sides:
                            pl.when((way == step) == (name == "inward"))(lambda: send_wide(step))
                elif name == "rows":
                    add_rows()
                elif name[0] == "z":
                    first(slot, int(name[2]), MODES[role][slot])
                elif name[0] == "d":
                    second(slot, int(name[2]), MODES[role][slot])
                elif name[0] == "r":
                    third(slot, MODES[role][slot])
                else:
                    handed(slot)

    head = jnp.logical_and(chip == 0, rep == 0)

    def by_role(i):
        if chips > 4:
            run(STEPS[RING][i], RING)
            return
        if STEPS[HEAD][i] == STEPS[EDGE][i]:
            pl.when(edge)(lambda: run(STEPS[EDGE][i], EDGE))
        else:
            pl.when(head)(lambda: run(STEPS[HEAD][i], EDGE))
            pl.when(jnp.logical_and(edge, lower(head)))(lambda: run(STEPS[EDGE][i], EDGE))
        pl.when(lower(edge))(lambda: run(STEPS[AMID][i], AMID))

    for h in range(2):
        for step in (1, -1):
            pl.when(lower(is_up(step)))(lambda: z_copy(step, h).start())
    partner_own.start()

    index_copy.wait()
    own_copy.wait()
    wanted = wanted_ref[...] - me * block_rows
    spots = lax.broadcasted_iota(jnp.int32, (block_rows, count), 0)
    onehot = (spots == wanted).astype(jnp.bfloat16)
    mine = lax.dot_general(
        onehot, win[0], (((0,), (0,)), ((), ())), preferred_element_type=jnp.float32
    )
    rows_ref[0] = mine[:, :half].astype(jnp.bfloat16)
    rows_ref[1] = mine[:, half:].astype(jnp.bfloat16)
    give_half.start()
    with jax.named_scope("half"):
        give_half.wait_recv()
    both = rows_ref[core].astype(jnp.float32) + heard[0].astype(jnp.float32)
    chip_ref[0] = both.astype(jnp.bfloat16)
    everywhere(lambda i: pl.when(lower(is_up(i)))(lambda: rows_out(i).start()))

    @pl.when(is_up(1))
    def _():
        with jax.named_scope("next"):
            pl.semaphore_wait(allow.at[0], 1)
        send_z(1, range(2))

    with jax.named_scope("allow"):
        allowed(2, rep_ups)
        allowed(3, ups)
    def body(i, carry):
        for j in range(3):
            pl.when(i == j)(lambda: by_role(j))

        @pl.when(i == 0)
        def _():
            with jax.named_scope("pivots"):
                swap.wait_recv()
                arrive(block_rows, o_recv.at[0])
            with jax.named_scope("scaled"):
                prepare()

        with jax.named_scope("cmp"):
            compare(lax.select(jnp.logical_and(lower(edge), i > 0), 3 - i, i) if chips <= 4 and SWAP else i)
        return carry

    lax.fori_loop(0, 3, body, 0)
    by_role(3)
    with jax.named_scope("drain"):
        relayed = sum(len(hops) for hops in relays.values()) * piece

        def total(role):
            rows = (3 if role == RING else 2) * part + 3 * block_rows + 3 * len(direct) * part
            for mode in MODES[role]:
                rows += relayed if mode == RELAY else len(diagonal) * part if mode == ROUTED else 0
            if role != RING:
                rows += sum(extra(role)) * len(diagonal) * part
            return rows + (2 * part if role == AMID else 0)

        if chips > 4:
            gone(total(RING))
        else:
            pl.when(edge)(lambda: gone(total(EDGE)))
            pl.when(lower(edge))(lambda: gone(total(AMID)))
        spot = heard.at[pl.ds(0, chips + 1)]
        remote(spot, spot, out_sem.at[1], p_recv.at[1], partner).wait_send()


def solution(mesh):
    n_vec, n_rep = mesh.shape["vec"], mesh.shape["rep"]
    n_b = 2 if n_rep % 2 == 0 else 1
    n_a = n_rep // n_b
    assert n_vec % 2 == 0 and n_vec > 2 * HALF

    def step(vectors, pivot_index):
        rows, fields = vectors.shape
        count = pivot_index.shape[1]
        dma = pltpu.SemaphoreType.DMA
        vmem = pl.BlockSpec(memory_space=pltpu.VMEM)
        hbm = pl.BlockSpec(memory_space=pltpu.HBM)
        held, win, scaled = pl.pallas_call(
            functools.partial(kernel, n_vec, n_a, n_b),
            out_shape=(
                pltpu.VMEM((2 * HALF + 1, count, rows, rows), jnp.bfloat16),
                pltpu.VMEM((7, rows, fields), jnp.bfloat16),
                pltpu.VMEM((count * rows, fields), jnp.bfloat16),
            ),
            in_specs=[hbm, hbm],
            out_specs=(vmem, vmem, vmem),
            scratch_shapes=[
                pltpu.VMEM((1, count), jnp.int32),
                pltpu.VMEM((2, count, fields // 2), jnp.bfloat16),
                pltpu.VMEM((2, count, fields // 2), jnp.bfloat16),
                pltpu.VMEM((n_vec // 2 + 1, count, fields // 2), jnp.bfloat16),
                dma((2,)), dma((2, 3)), dma((2,)), dma((3, 2)), dma((3,)), dma((3,)), dma((2,)),
                dma((1,)), dma((2,)), pltpu.SemaphoreType.REGULAR((4,)),
            ],
            compiler_params=pltpu.CompilerParams(
                collective_id=0, has_side_effects=True, vmem_limit_bytes=60_800_000
            ),
        )(vectors, pivot_index)
        return pl.pallas_call(
            functools.partial(closing, n_vec),
            out_shape=jax.ShapeDtypeStruct(held.shape, held.dtype),
            in_specs=[vmem, vmem, vmem],
            out_specs=pl.BlockSpec(memory_space=pl.ANY),
            scratch_shapes=[pltpu.VMEM((2, *held.shape[1:]), held.dtype), dma((2 * HALF + 3, CHUNKS))],
            compiler_params=pltpu.CompilerParams(vmem_limit_bytes=24 * 2**20),
        )(held, win, scaled)

    return jax.shard_map(
        step, mesh=mesh, in_specs=(P("vec", None), P("rep", None)),
        out_specs=P(None, "rep", "vec", None), check_vma=False,
    )
```

```python
import functools
import math

import jax
import jax.numpy as jnp
from jax import lax
from jax.experimental import pallas as pl
from jax.experimental.pallas import tpu as pltpu
from jax.sharding import PartitionSpec as P

HALF = 3
NEAR, OUTER, FAR = 0, 1, 2
AT = (3, 5, 2)
LAST = FAR
RELAY, ROUTED, WIDE = range(3)
EDGE, AMID, RING, HEAD = range(4)
def words(*parts):
    return " ".join(parts)


MODES = ((RELAY, WIDE, ROUTED), (RELAY, WIDE, ROUTED), (RELAY, RELAY, RELAY))
STEPS = {
    HEAD: (words("up z00 z01 inward", "outward z10 d00 d01", "z11 z20 z21 rows"), words("r0 d10 d11 r1", "h0"), words("h1"), words("d20 d21 r2")),
    EDGE: (words("up z00 z01 inward", "outward z10 d00 d01", "z11 z20 z21 rows"), words("r0 d10 d11 r1", "h0"), words("h1"), words("d20 d21 r2")),
    AMID: (words("up z00 z10 z11", "z01 outward d00 d01", "z20 z21 r1 d10", "d11 rows"), words("h1"), words("r0 h0"), words("d20 d21 r2")),
    RING: (words("z00 z10 z01 z11", "up d00 d01 rows", "z20 z21 d10 d11", "r0 d20 d21 r1"), words("h0"), words("h1"), words("r2")),
}
CHUNKS = 1
SWAP = True
SIDES = (-1, 1)


def contract(left, right):
    return lax.dot_general(
        left, right, (((1,), (1,)), ((), ())), preferred_element_type=jnp.float32
    )


def inward(chip, chips):
    return 1 - 2 * (2 * chip // chips) if chips <= 4 else 1 + 0 * chip


def pairs(i, core, way):
    if isinstance(i, int) and i == 3 and LAST == FAR:
        return 1, HALF + 1 - 2 * core, 2 * HALF * core
    if isinstance(i, int) and i == 3:
        return 5, HALF - 2 * way, HALF - 2 * way + 1 - 2 * core
    if LAST == FAR:
        step = way * (i % 2) - way * (i // 2)
        mine = HALF + 2 * step
        return (i > 0) + 2 * i, mine, mine + 1 - 2 * core
    near, far = i % 2, i // 2
    mine = HALF + 2 * way * near + far * (1 - 2 * core)
    other = (HALF + 2 * way * near + 1 - 2 * core) * (1 - far) + 2 * HALF * core * far
    return 3 * near + far, mine, other


def products(scaled, right, count):
    value = (contract(scaled, right) * (1.0 / math.sqrt(scaled.shape[1]))).astype(jnp.bfloat16)
    return value.reshape(count, scaled.shape[0] // count, right.shape[0])


def closing(n_vec, held, win, scaled, out_ref, last, sems):
    window, count, block_rows, fields = held.shape[0], held.shape[1], held.shape[2], win.shape[2]
    me = lax.axis_index("vec")
    base, first, second = pairs(3, me % 2, inward(me // 2, n_vec // 2))
    fresh = [second] if LAST == FAR else [first, second]

    def ready(i):
        return pltpu.make_async_copy(held.at[i], out_ref.at[i], sems.at[i, 0])

    some = count // CHUNKS

    def late(j, n):
        ks = pl.ds(n * some, some)
        return pltpu.make_async_copy(last.at[j, ks], out_ref.at[fresh[j], ks], sems.at[window + j, n])

    def others(action):
        for i in range(window):
            unlike = fresh[0] != i
            for spot in fresh[1:]:
                unlike = jnp.logical_and(unlike, spot != i)
            pl.when(unlike)(lambda i=i: action(i))

    with jax.named_scope("s"):
        others(lambda i: ready(i).start())
    right = win[base:base + 2].reshape(2 * block_rows, fields)
    for n in range(CHUNKS):
        with jax.named_scope(f"c{n}"):
            value = products(scaled[n * some * block_rows:(n + 1) * some * block_rows], right, some)
            for j in range(len(fresh)):
                h = 2 - len(fresh) + j
                last[j, n * some:(n + 1) * some] = value[:, :, h * block_rows:(h + 1) * block_rows]
                late(j, n).start()
    with jax.named_scope("w0"):
        others(lambda i: ready(i).wait())
    with jax.named_scope("w1"):
        for j in range(len(fresh)):
            for n in range(CHUNKS):
                late(j, n).wait()


def kernel(
    n_vec, n_a, n_b, vec_ref, index_ref, out_ref, win, scaled, wanted_ref, rows_ref, chip_ref, heard,
    out_sem, z_recv, f_recv, d_recv, r_recv, p_recv, h_recv, o_recv, local_sem, allow,
):
    block_rows, fields = vec_ref.shape
    count = index_ref.shape[1]
    n_rep = n_a * n_b
    chips = n_vec // 2
    part = block_rows // n_rep
    piece = part // 2
    me = lax.axis_index("vec")
    rep = lax.axis_index("rep")
    a, b = rep // n_b, rep % n_b
    chip, core = me // 2, me % 2
    partner = {"vec": me + 1 - 2 * core}
    way = inward(chip, chips)
    short = n_vec <= 16

    def chip_index(offset):
        return (chip + offset + chips) % chips

    def at_chip(offset, which):
        return {"vec": 2 * chip_index(offset) + which}

    def rep_of(da, db):
        return ((a + da + n_a) % n_a) * n_b + (b + db + n_b) % n_b

    direct = [(0, i) for i in range(1, n_b)] + [(i, 0) for i in range(1, n_a)]
    diagonal = [(i, j) for i in range(1, n_a) for j in range(1, n_b)]
    relays = {}
    for t, (da, db) in enumerate(direct):
        if da == 0:
            relays[t] = [((i, 0), diagonal.index((i, db))) for i in range(1, n_a)]
        else:
            relays[t] = [((0, j), diagonal.index((da, j))) for j in range(1, n_b)]
    side = [0 if da == 0 else 1 for da, _ in direct]

    own_copy = pltpu.make_async_copy(vec_ref, win.at[0], local_sem.at[0])
    index_copy = pltpu.make_async_copy(index_ref, wanted_ref, local_sem.at[1])
    own_copy.start()
    index_copy.start()

    def is_up(offset):
        return chip_index(offset) > chip

    def rep_is_up(da, db):
        return rep_of(da, db) > rep

    def number_of(flags):
        return sum((flag.astype(jnp.int32) for flag in flags), jnp.int32(0))

    def everywhere(action):
        def body(i, carry):
            action(i)
            return carry

        lax.fori_loop(1, chips, body, 0, unroll=short)

    barrier = pltpu.get_barrier_semaphore()
    lower = jnp.logical_not

    def meet(sem, when, device):
        pl.when(when)(lambda: pl.semaphore_signal(sem, inc=1, device_id=device))

    def allowed(i, times):
        pl.when(times > 0)(lambda: pl.semaphore_wait(allow.at[i], times))

    sides = (1, -1)
    everywhere(lambda i: meet(barrier, is_up(i), at_chip(i, core)))
    for step in sides:
        meet(barrier, is_up(step), at_chip(step, 1 - core))
    for hop in direct:
        meet(barrier, rep_is_up(*hop), {"rep": rep_of(*hop)})
    pl.semaphore_signal(barrier, inc=1, device_id=partner)
    ups = number_of([is_up(step) for step in sides])
    rep_ups = number_of([rep_is_up(*hop) for hop in direct])
    with jax.named_scope("barrier"):
        pl.semaphore_wait(barrier, chip + (2 - ups) + (len(direct) - rep_ups) + 1)
    meet(allow.at[0], lower(is_up(-1)), at_chip(-1, core))
    everywhere(lambda i: meet(allow.at[1], lower(is_up(i)), at_chip(i, core)))
    for hop in direct:
        meet(allow.at[2], lower(rep_is_up(*hop)), {"rep": rep_of(*hop)})
    for step in sides:
        meet(allow.at[3], lower(is_up(step)), at_chip(step, 1 - core))

    def remote(src, dst, send_sem, recv_sem, device):
        return pltpu.make_async_remote_copy(
            src_ref=src, dst_ref=dst, send_sem=send_sem, recv_sem=recv_sem, device_id=device
        )

    def arrive(rows, sem):
        spot = scaled.at[pl.ds(0, rows)]
        remote(spot, spot, out_sem.at[0], sem, partner).wait_recv()

    def gone(rows):
        spot = scaled.at[pl.ds(0, rows)]
        remote(spot, spot, out_sem.at[0], o_recv.at[0], partner).wait_send()

    def rows_at(which, h):
        return pl.ds(pl.multiple_of(which * part + h * piece, piece), piece)

    def quarter(da, db, h):
        return rows_at(rep_of(-da, -db), h)

    own = [rows_at(rep, h) for h in range(2)]

    if chips <= 4:
        edge = jnp.logical_or(chip == 0, chip == chips - 1)
    else:
        edge = chip < 0

    def z_copy(step, which):
        looks = inward(chip_index(step), chips)
        slot = (1 + step * looks) // 2
        if which < 2:
            rows = own[which]
        else:
            rows = pl.ds(pl.multiple_of(rep_of(*diagonal[which - 2]) * part, part), part)
        return remote(
            vec_ref.at[rows], win.at[AT[NEAR] + (AT[OUTER] - AT[NEAR]) * slot, rows],
            out_sem.at[0], z_recv.at[slot, jnp.minimum(which, 2)], at_chip(step, core),
        )

    def passes(slot):
        return lower(edge) if chips <= 4 else core == slot

    def pass_on(slot, h):
        step = -way if slot == NEAR else way
        return remote(
            win.at[AT[slot], own[h]], win.at[AT[FAR], own[h]], out_sem.at[0], f_recv.at[h],
            at_chip(step, 1 - core),
        )

    def d_copy(slot, t, h):
        spot = win.at[AT[slot], own[h]]
        return remote(spot, spot, out_sem.at[0], d_recv.at[slot, h], {"rep": rep_of(*direct[t])})

    def routed_copy(slot, number, h):
        spot = win.at[AT[slot], own[h]]
        return remote(spot, spot, out_sem.at[0], r_recv.at[slot], {"rep": rep_of(*diagonal[number])})

    def r_copy(slot, t, hop):
        spot = win.at[AT[slot], quarter(*direct[t], side[t])]
        return remote(spot, spot, out_sem.at[0], r_recv.at[slot], {"rep": rep_of(*hop)})

    def hand(slot, rows):
        if slot != FAR:
            remote(
                win.at[AT[slot], rows], win.at[AT[slot] + 1, rows], out_sem.at[0], h_recv.at[slot], partner
            ).start()

    def handed(slot):
        arrive(block_rows, h_recv.at[slot])

    half = fields // 2

    def halves(src, dst, k, device):
        return remote(src, heard.at[dst], out_sem.at[1], p_recv.at[k], device)

    give_half = halves(rows_ref.at[1 - core], 0, 0, partner)
    swap = halves(chip_ref.at[1], chips, 2, partner)

    def rows_out(i):
        return halves(chip_ref.at[0], i, 1, at_chip(i, core))

    def first(slot, h, mode):
        arrive(piece, f_recv.at[h] if slot == FAR else z_recv.at[slot, h])
        if slot != FAR:
            pl.when(passes(slot))(lambda: pass_on(slot, h).start())
        if mode == ROUTED:
            for number in range(len(diagonal)):
                routed_copy(slot, number, h).start()
        for t in range(len(direct)):
            d_copy(slot, t, h).start()
        hand(slot, own[h])

    def second(slot, h, mode):
        if direct:
            arrive(len(direct) * piece, d_recv.at[slot, h])
        for t in range(len(direct)):
            if side[t] == h and mode == RELAY:
                for hop, number in relays[t]:
                    r_copy(slot, t, hop).start()
            hand(slot, quarter(*direct[t], h))

    def third(slot, mode):
        if diagonal:
            arrive(len(diagonal) * part, z_recv.at[slot, 2] if mode == WIDE else r_recv.at[slot])
        for spot in diagonal:
            for h in range(2):
                hand(slot, quarter(*spot, h))

    partner_own = remote(vec_ref, win.at[1], out_sem.at[0], o_recv.at[0], partner)

    def prepare():
        mine, other = chip_ref[1].astype(jnp.float32), heard[chips].astype(jnp.float32)
        pivots = jnp.concatenate(
            [jnp.where(core == 0, mine, other), jnp.where(core == 0, other, mine)], axis=1
        )
        level = jnp.sum(pivots, axis=1, keepdims=True) / fields
        pivots = pivots - level
        block = win[0].astype(jnp.float32)
        for k in range(count):
            scaled[k * block_rows:(k + 1) * block_rows, :] = (block * pivots[k:k + 1, :]).astype(jnp.bfloat16)

    def compare(i):
        base, mine_at, other_at = pairs(i, core, way)
        value = products(scaled[...], win[pl.ds(base, 2)].reshape(2 * block_rows, fields), count)
        out_ref[mine_at] = value[:, :, :block_rows]
        out_ref[other_at] = value[:, :, block_rows:]

    def send_z(step, steps):
        for which in steps:
            z_copy(step, which).start()

    def send_wide(step):
        if diagonal:
            send_z(step, range(2, 2 + len(diagonal)))

    def extra(role):
        if role == EDGE:
            return MODES[AMID][OUTER] == WIDE, MODES[EDGE][OUTER] == WIDE
        return MODES[AMID][NEAR] == WIDE, MODES[EDGE][NEAR] == WIDE

    def up():
        allowed(1, chips - 1 - chip)
        pl.when(is_up(-1))(lambda: send_z(-1, range(2)))
        everywhere(lambda i: pl.when(is_up(i))(lambda: rows_out(i).start()))

    def add_rows():
        spot = heard.at[pl.ds(1, chips - 1)]
        remote(spot, spot, out_sem.at[1], p_recv.at[1], partner).wait_recv()
        total = lax.fori_loop(
            1, chips, lambda i, total: total + heard[i].astype(jnp.float32),
            chip_ref[0].astype(jnp.float32), unroll=short,
        )
        chip_ref[1] = total.astype(jnp.bfloat16)
        swap.start()

    def run(steps, role):
        for name in steps.split():
            slot = int(name[1]) if name[1].isdigit() else None
            with jax.named_scope(name):
                if name == "up":
                    up()
                elif name in ("inward", "outward"):
                    if extra(role)[name == "outward"]:
                        for step in sides:
                            pl.when((way == step) == (name == "inward"))(lambda: send_wide(step))
                elif name == "rows":
                    add_rows()
                elif name[0] == "z":
                    first(slot, int(name[2]), MODES[role][slot])
                elif name[0] == "d":
                    second(slot, int(name[2]), MODES[role][slot])
                elif name[0] == "r":
                    third(slot, MODES[role][slot])
                else:
                    handed(slot)

    head = jnp.logical_and(chip == 0, rep == 0)

    def by_role(i):
        if chips > 4:
            run(STEPS[RING][i], RING)
            return
        if STEPS[HEAD][i] == STEPS[EDGE][i]:
            pl.when(edge)(lambda: run(STEPS[EDGE][i], EDGE))
        else:
            pl.when(head)(lambda: run(STEPS[HEAD][i], EDGE))
            pl.when(jnp.logical_and(edge, lower(head)))(lambda: run(STEPS[EDGE][i], EDGE))
        pl.when(lower(edge))(lambda: run(STEPS[AMID][i], AMID))

    for h in range(2):
        for step in SIDES:
            pl.when(lower(is_up(step)))(lambda: z_copy(step, h).start())
    partner_own.start()

    index_copy.wait()
    own_copy.wait()
    wanted = wanted_ref[...] - me * block_rows
    spots = lax.broadcasted_iota(jnp.int32, (block_rows, count), 0)
    onehot = (spots == wanted).astype(jnp.bfloat16)
    mine = lax.dot_general(
        onehot, win[0], (((0,), (0,)), ((), ())), preferred_element_type=jnp.float32
    )
    rows_ref[0] = mine[:, :half].astype(jnp.bfloat16)
    rows_ref[1] = mine[:, half:].astype(jnp.bfloat16)
    give_half.start()
    with jax.named_scope("half"):
        give_half.wait_recv()
    both = rows_ref[core].astype(jnp.float32) + heard[0].astype(jnp.float32)
    chip_ref[0] = both.astype(jnp.bfloat16)
    everywhere(lambda i: pl.when(lower(is_up(i)))(lambda: rows_out(i).start()))

    @pl.when(is_up(1))
    def _():
        with jax.named_scope("next"):
            pl.semaphore_wait(allow.at[0], 1)
        send_z(1, range(2))

    with jax.named_scope("allow"):
        allowed(2, rep_ups)
        allowed(3, ups)
    def body(i, carry):
        for j in range(3):
            pl.when(i == j)(lambda: by_role(j))

        @pl.when(i == 0)
        def _():
            with jax.named_scope("pivots"):
                swap.wait_recv()
                arrive(block_rows, o_recv.at[0])
            with jax.named_scope("scaled"):
                prepare()

        with jax.named_scope("cmp"):
            compare(lax.select(jnp.logical_and(lower(edge), i > 0), 3 - i, i) if chips <= 4 and SWAP else i)
        return carry

    lax.fori_loop(0, 3, body, 0)
    by_role(3)
    with jax.named_scope("drain"):
        relayed = sum(len(hops) for hops in relays.values()) * piece

        def total(role):
            rows = (3 if role == RING else 2) * part + 3 * block_rows + 3 * len(direct) * part
            for mode in MODES[role]:
                rows += relayed if mode == RELAY else len(diagonal) * part if mode == ROUTED else 0
            if role != RING:
                rows += sum(extra(role)) * len(diagonal) * part
            return rows + (2 * part if role == AMID else 0)

        if chips > 4:
            gone(total(RING))
        else:
            pl.when(edge)(lambda: gone(total(EDGE)))
            pl.when(lower(edge))(lambda: gone(total(AMID)))
        spot = heard.at[pl.ds(0, chips + 1)]
        remote(spot, spot, out_sem.at[1], p_recv.at[1], partner).wait_send()


def solution(mesh):
    n_vec, n_rep = mesh.shape["vec"], mesh.shape["rep"]
    n_b = 2 if n_rep % 2 == 0 else 1
    n_a = n_rep // n_b
    assert n_vec % 2 == 0 and n_vec > 2 * HALF

    def step(vectors, pivot_index):
        rows, fields = vectors.shape
        count = pivot_index.shape[1]
        dma = pltpu.SemaphoreType.DMA
        vmem = pl.BlockSpec(memory_space=pltpu.VMEM)
        hbm = pl.BlockSpec(memory_space=pltpu.HBM)
        held, win, scaled = pl.pallas_call(
            functools.partial(kernel, n_vec, n_a, n_b),
            out_shape=(
                pltpu.VMEM((2 * HALF + 1, count, rows, rows), jnp.bfloat16),
                pltpu.VMEM((7, rows, fields), jnp.bfloat16),
                pltpu.VMEM((count * rows, fields), jnp.bfloat16),
            ),
            in_specs=[hbm, hbm],
            out_specs=(vmem, vmem, vmem),
            scratch_shapes=[
                pltpu.VMEM((1, count), jnp.int32),
                pltpu.VMEM((2, count, fields // 2), jnp.bfloat16),
                pltpu.VMEM((2, count, fields // 2), jnp.bfloat16),
                pltpu.VMEM((n_vec // 2 + 1, count, fields // 2), jnp.bfloat16),
                dma((2,)), dma((2, 3)), dma((2,)), dma((3, 2)), dma((3,)), dma((3,)), dma((2,)),
                dma((1,)), dma((2,)), pltpu.SemaphoreType.REGULAR((4,)),
            ],
            compiler_params=pltpu.CompilerParams(
                collective_id=0, has_side_effects=True, vmem_limit_bytes=60_800_000
            ),
        )(vectors, pivot_index)
        return pl.pallas_call(
            functools.partial(closing, n_vec),
            out_shape=jax.ShapeDtypeStruct(held.shape, held.dtype),
            in_specs=[vmem, vmem, vmem],
            out_specs=pl.BlockSpec(memory_space=pl.ANY),
            scratch_shapes=[pltpu.VMEM((2, *held.shape[1:]), held.dtype), dma((2 * HALF + 3, CHUNKS))],
            compiler_params=pltpu.CompilerParams(vmem_limit_bytes=24 * 2**20),
        )(held, win, scaled)

    return jax.shard_map(
        step, mesh=mesh, in_specs=(P("vec", None), P("rep", None)),
        out_specs=P(None, "rep", "vec", None), check_vma=False,
    )
```

```python
import functools
import math

import jax
import jax.numpy as jnp
from jax import lax
from jax.experimental import pallas as pl
from jax.experimental.pallas import tpu as pltpu
from jax.sharding import PartitionSpec as P

HALF = 3
NEAR, OUTER, FAR = 0, 1, 2
AT = (3, 5, 2)
LAST = FAR
RELAY, ROUTED, WIDE = range(3)
LOW_END, LOW_MID, HIGH_MID, HIGH_END, RING = range(5)
ACROSS = (HIGH_END, HIGH_MID, LOW_MID, LOW_END)
BESIDE = (LOW_MID, LOW_END, HIGH_END, HIGH_MID)
MODES = (
    (RELAY, WIDE, WIDE),
    (WIDE, WIDE, ROUTED),
    (RELAY, WIDE, ROUTED),
    (RELAY, WIDE, ROUTED),
    (RELAY, RELAY, RELAY),
)


def words(*parts):
    return " ".join(parts)


STEPS = (
    (
        words("up z00 z01 inward", "outward z10 d00 d01", "z11 z20 z21 rows"),
        words("r0 d10 d11 r1", "h0"),
        words("h1"),
        words("d20 d21 r2"),
    ),
    (
        words("up z00 z10 z11", "z01 d00 d01 r0", "z20 z21 r1 d10", "d11 rows"),
        words("h1"),
        words("h0"),
        words("d20 d21 r2"),
    ),
    (
        words("up inward z00 z10", "z11 z01 d00 d01", "z20 z21 r1 d10", "d11 rows"),
        words("h1"),
        words("r0 h0"),
        words("d20 d21 r2"),
    ),
    (
        words("up z00 z01 inward", "outward z10 d00 d01", "z11 z20 z21 rows"),
        words("r0 d10 d11 r1", "h0"),
        words("h1"),
        words("d20 d21 r2"),
    ),
    (
        words("z00 z10 z01 z11", "up d00 d01 rows", "z20 z21 d10 d11", "r0 d20 d21 r1"),
        words("h0"),
        words("h1"),
        words("r2"),
    ),
)
CHUNKS = 1
SWAP = True
SIDES = (-1, 1)


def contract(left, right):
    return lax.dot_general(
        left, right, (((1,), (1,)), ((), ())), preferred_element_type=jnp.float32
    )


def inward(chip, chips):
    return 1 - 2 * (2 * chip // chips) if chips == 4 else 1 + 0 * chip


def pairs(i, core, way):
    if isinstance(i, int) and i == 3 and LAST == FAR:
        return 1, HALF + 1 - 2 * core, 2 * HALF * core
    if isinstance(i, int) and i == 3:
        return 5, HALF - 2 * way, HALF - 2 * way + 1 - 2 * core
    if LAST == FAR:
        step = way * (i % 2) - way * (i // 2)
        mine = HALF + 2 * step
        return (i > 0) + 2 * i, mine, mine + 1 - 2 * core
    near, far = i % 2, i // 2
    mine = HALF + 2 * way * near + far * (1 - 2 * core)
    other = (HALF + 2 * way * near + 1 - 2 * core) * (1 - far) + 2 * HALF * core * far
    return 3 * near + far, mine, other


def products(scaled, right, count):
    value = (contract(scaled, right) * (1.0 / math.sqrt(scaled.shape[1]))).astype(jnp.bfloat16)
    return value.reshape(count, scaled.shape[0] // count, right.shape[0])


def closing(n_vec, held, win, scaled, out_ref, last, sems):
    window, count, block_rows, fields = held.shape[0], held.shape[1], held.shape[2], win.shape[2]
    me = lax.axis_index("vec")
    base, first, second = pairs(3, me % 2, inward(me // 2, n_vec // 2))
    fresh = [second] if LAST == FAR else [first, second]

    def ready(i):
        return pltpu.make_async_copy(held.at[i], out_ref.at[i], sems.at[i, 0])

    some = count // CHUNKS

    def late(j, n):
        ks = pl.ds(n * some, some)
        return pltpu.make_async_copy(last.at[j, ks], out_ref.at[fresh[j], ks], sems.at[window + j, n])

    def others(action):
        for i in range(window):
            unlike = fresh[0] != i
            for spot in fresh[1:]:
                unlike = jnp.logical_and(unlike, spot != i)
            pl.when(unlike)(lambda i=i: action(i))

    with jax.named_scope("s"):
        others(lambda i: ready(i).start())
    right = win[base:base + 2].reshape(2 * block_rows, fields)
    for n in range(CHUNKS):
        with jax.named_scope(f"c{n}"):
            value = products(scaled[n * some * block_rows:(n + 1) * some * block_rows], right, some)
            for j in range(len(fresh)):
                h = 2 - len(fresh) + j
                last[j, n * some:(n + 1) * some] = value[:, :, h * block_rows:(h + 1) * block_rows]
                late(j, n).start()
    with jax.named_scope("w0"):
        others(lambda i: ready(i).wait())
    with jax.named_scope("w1"):
        for j in range(len(fresh)):
            for n in range(CHUNKS):
                late(j, n).wait()


def kernel(
    n_vec, n_a, n_b, vec_ref, index_ref, out_ref, win, scaled, wanted_ref, rows_ref, chip_ref, heard,
    out_sem, z_recv, f_recv, d_recv, r_recv, p_recv, h_recv, o_recv, local_sem, allow,
):
    block_rows, fields = vec_ref.shape
    count = index_ref.shape[1]
    n_rep = n_a * n_b
    chips = n_vec // 2
    part = block_rows // n_rep
    piece = part // 2
    me = lax.axis_index("vec")
    rep = lax.axis_index("rep")
    a, b = rep // n_b, rep % n_b
    chip, core = me // 2, me % 2
    partner = {"vec": me + 1 - 2 * core}
    way = inward(chip, chips)
    short = n_vec <= 16

    def chip_index(offset):
        return (chip + offset + chips) % chips

    def at_chip(offset, which):
        return {"vec": 2 * chip_index(offset) + which}

    def rep_of(da, db):
        return ((a + da + n_a) % n_a) * n_b + (b + db + n_b) % n_b

    direct = [(0, i) for i in range(1, n_b)] + [(i, 0) for i in range(1, n_a)]
    diagonal = [(i, j) for i in range(1, n_a) for j in range(1, n_b)]
    relays = {}
    for t, (da, db) in enumerate(direct):
        if da == 0:
            relays[t] = [((i, 0), diagonal.index((i, db))) for i in range(1, n_a)]
        else:
            relays[t] = [((0, j), diagonal.index((da, j))) for j in range(1, n_b)]
    side = [0 if da == 0 else 1 for da, _ in direct]

    own_copy = pltpu.make_async_copy(vec_ref, win.at[0], local_sem.at[0])
    index_copy = pltpu.make_async_copy(index_ref, wanted_ref, local_sem.at[1])
    own_copy.start()
    index_copy.start()

    def is_up(offset):
        return chip_index(offset) > chip

    def rep_is_up(da, db):
        return rep_of(da, db) > rep

    def number_of(flags):
        return sum((flag.astype(jnp.int32) for flag in flags), jnp.int32(0))

    def everywhere(action):
        def body(i, carry):
            action(i)
            return carry

        lax.fori_loop(1, chips, body, 0, unroll=short)

    barrier = pltpu.get_barrier_semaphore()
    lower = jnp.logical_not

    def meet(sem, when, device):
        pl.when(when)(lambda: pl.semaphore_signal(sem, inc=1, device_id=device))

    def allowed(i, times):
        pl.when(times > 0)(lambda: pl.semaphore_wait(allow.at[i], times))

    sides = (1, -1)
    everywhere(lambda i: meet(barrier, is_up(i), at_chip(i, core)))
    for step in sides:
        meet(barrier, is_up(step), at_chip(step, 1 - core))
    for hop in direct:
        meet(barrier, rep_is_up(*hop), {"rep": rep_of(*hop)})
    pl.semaphore_signal(barrier, inc=1, device_id=partner)
    ups = number_of([is_up(step) for step in sides])
    rep_ups = number_of([rep_is_up(*hop) for hop in direct])
    with jax.named_scope("barrier"):
        pl.semaphore_wait(barrier, chip + (2 - ups) + (len(direct) - rep_ups) + 1)
    meet(allow.at[0], lower(is_up(-1)), at_chip(-1, core))
    everywhere(lambda i: meet(allow.at[1], lower(is_up(i)), at_chip(i, core)))
    for hop in direct:
        meet(allow.at[2], lower(rep_is_up(*hop)), {"rep": rep_of(*hop)})
    for step in sides:
        meet(allow.at[3], lower(is_up(step)), at_chip(step, 1 - core))

    def remote(src, dst, send_sem, recv_sem, device):
        return pltpu.make_async_remote_copy(
            src_ref=src, dst_ref=dst, send_sem=send_sem, recv_sem=recv_sem, device_id=device
        )

    def arrive(rows, sem):
        spot = scaled.at[pl.ds(0, rows)]
        remote(spot, spot, out_sem.at[0], sem, partner).wait_recv()

    def gone(rows):
        spot = scaled.at[pl.ds(0, rows)]
        remote(spot, spot, out_sem.at[0], o_recv.at[0], partner).wait_send()

    def rows_at(which, h):
        return pl.ds(pl.multiple_of(which * part + h * piece, piece), piece)

    def quarter(da, db, h):
        return rows_at(rep_of(-da, -db), h)

    own = [rows_at(rep, h) for h in range(2)]

    if chips == 4:
        edge = jnp.logical_or(chip == 0, chip == chips - 1)
    else:
        edge = chip < 0

    def z_copy(step, which):
        looks = inward(chip_index(step), chips)
        slot = (1 + step * looks) // 2
        if which < 2:
            rows = own[which]
        else:
            rows = pl.ds(pl.multiple_of(rep_of(*diagonal[which - 2]) * part, part), part)
        return remote(
            vec_ref.at[rows], win.at[AT[NEAR] + (AT[OUTER] - AT[NEAR]) * slot, rows],
            out_sem.at[0], z_recv.at[slot, jnp.minimum(which, 2)], at_chip(step, core),
        )

    def passes(slot):
        return lower(edge) if chips == 4 else core == slot

    def pass_on(slot, h):
        step = -way if slot == NEAR else way
        return remote(
            win.at[AT[slot], own[h]], win.at[AT[FAR], own[h]], out_sem.at[0], f_recv.at[h],
            at_chip(step, 1 - core),
        )

    def d_copy(slot, t, h):
        spot = win.at[AT[slot], own[h]]
        return remote(spot, spot, out_sem.at[0], d_recv.at[slot, h], {"rep": rep_of(*direct[t])})

    def routed_copy(slot, number, h):
        spot = win.at[AT[slot], own[h]]
        return remote(spot, spot, out_sem.at[0], r_recv.at[slot], {"rep": rep_of(*diagonal[number])})

    def r_copy(slot, t, hop):
        spot = win.at[AT[slot], quarter(*direct[t], side[t])]
        return remote(spot, spot, out_sem.at[0], r_recv.at[slot], {"rep": rep_of(*hop)})

    def hand(slot, rows):
        if slot != FAR:
            remote(
                win.at[AT[slot], rows], win.at[AT[slot] + 1, rows], out_sem.at[0], h_recv.at[slot], partner
            ).start()

    def handed(slot):
        arrive(block_rows, h_recv.at[slot])

    half = fields // 2

    def halves(src, dst, k, device):
        return remote(src, heard.at[dst], out_sem.at[1], p_recv.at[k], device)

    give_half = halves(rows_ref.at[1 - core], 0, 0, partner)
    swap = halves(chip_ref.at[1], chips, 2, partner)

    def rows_out(i):
        return halves(chip_ref.at[0], i, 1, at_chip(i, core))

    def first(slot, h, mode):
        arrive(piece, f_recv.at[h] if slot == FAR else z_recv.at[slot, h])
        if slot != FAR:
            pl.when(passes(slot))(lambda: pass_on(slot, h).start())
        if mode == ROUTED:
            for number in range(len(diagonal)):
                routed_copy(slot, number, h).start()
        for t in range(len(direct)):
            d_copy(slot, t, h).start()
        hand(slot, own[h])

    def second(slot, h, mode):
        if direct:
            arrive(len(direct) * piece, d_recv.at[slot, h])
        for t in range(len(direct)):
            if side[t] == h and mode == RELAY:
                for hop, number in relays[t]:
                    r_copy(slot, t, hop).start()
            hand(slot, quarter(*direct[t], h))

    def third(slot, mode, role):
        if diagonal:
            if mode != WIDE:
                sem = r_recv.at[slot]
            else:
                sem = f_recv.at[2] if slot == FAR else z_recv.at[slot, 2]
            arrive(len(diagonal) * part, sem)
        if slot == NEAR and widens(role):
            for spot in diagonal:
                rows = pl.ds(pl.multiple_of(rep_of(*spot) * part, part), part)
                remote(
                    win.at[AT[NEAR], rows], win.at[AT[FAR], rows], out_sem.at[0], f_recv.at[2],
                    at_chip(-way, 1 - core),
                ).start()
        for spot in diagonal:
            for h in range(2):
                hand(slot, quarter(*spot, h))

    partner_own = remote(vec_ref, win.at[1], out_sem.at[0], o_recv.at[0], partner)

    def prepare():
        mine, other = chip_ref[1].astype(jnp.float32), heard[chips].astype(jnp.float32)
        pivots = jnp.concatenate(
            [jnp.where(core == 0, mine, other), jnp.where(core == 0, other, mine)], axis=1
        )
        level = jnp.sum(pivots, axis=1, keepdims=True) / fields
        pivots = pivots - level
        block = win[0].astype(jnp.float32)
        for k in range(count):
            scaled[k * block_rows:(k + 1) * block_rows, :] = (block * pivots[k:k + 1, :]).astype(jnp.bfloat16)

    def compare(i):
        base, mine_at, other_at = pairs(i, core, way)
        value = products(scaled[...], win[pl.ds(base, 2)].reshape(2 * block_rows, fields), count)
        out_ref[mine_at] = value[:, :, :block_rows]
        out_ref[other_at] = value[:, :, block_rows:]

    def send_z(step, steps):
        for which in steps:
            z_copy(step, which).start()

    def send_wide(step):
        if diagonal:
            send_z(step, range(2, 2 + len(diagonal)))

    def extra(role):
        ends = role in (LOW_END, HIGH_END)
        inside = MODES[BESIDE[role]][OUTER] if ends else MODES[ACROSS[role]][NEAR]
        outside = MODES[ACROSS[role]][OUTER] if ends else MODES[BESIDE[role]][NEAR]
        return inside == WIDE, outside == WIDE

    def widens(role):
        return role in (LOW_MID, HIGH_MID) and MODES[BESIDE[role]][FAR] == WIDE

    def up():
        allowed(1, chips - 1 - chip)
        pl.when(is_up(-1))(lambda: send_z(-1, range(2)))
        everywhere(lambda i: pl.when(is_up(i))(lambda: rows_out(i).start()))

    def add_rows():
        spot = heard.at[pl.ds(1, chips - 1)]
        remote(spot, spot, out_sem.at[1], p_recv.at[1], partner).wait_recv()
        total = lax.fori_loop(
            1, chips, lambda i, total: total + heard[i].astype(jnp.float32),
            chip_ref[0].astype(jnp.float32), unroll=short,
        )
        chip_ref[1] = total.astype(jnp.bfloat16)
        swap.start()

    def run(steps, role):
        for name in steps.split():
            slot = int(name[1]) if name[1].isdigit() else None
            with jax.named_scope(name):
                if name == "up":
                    up()
                elif name in ("inward", "outward"):
                    if extra(role)[name == "outward"]:
                        for step in sides:
                            pl.when((way == step) == (name == "inward"))(lambda: send_wide(step))
                elif name == "rows":
                    add_rows()
                elif name[0] == "z":
                    first(slot, int(name[2]), MODES[role][slot])
                elif name[0] == "d":
                    second(slot, int(name[2]), MODES[role][slot])
                elif name[0] == "r":
                    third(slot, MODES[role][slot], role)
                else:
                    handed(slot)

    is_role = [chip == 0, chip == 1, chip == 2, chip == 3]

    def by_role(i):
        if chips != 4:
            run(STEPS[RING][i], RING)
            return
        for role in range(chips):
            pl.when(is_role[role])(lambda: run(STEPS[role][i], role))

    for h in range(2):
        for step in SIDES:
            pl.when(lower(is_up(step)))(lambda: z_copy(step, h).start())
    partner_own.start()

    index_copy.wait()
    own_copy.wait()
    wanted = wanted_ref[...] - me * block_rows
    spots = lax.broadcasted_iota(jnp.int32, (block_rows, count), 0)
    onehot = (spots == wanted).astype(jnp.bfloat16)
    mine = lax.dot_general(
        onehot, win[0], (((0,), (0,)), ((), ())), preferred_element_type=jnp.float32
    )
    rows_ref[0] = mine[:, :half].astype(jnp.bfloat16)
    rows_ref[1] = mine[:, half:].astype(jnp.bfloat16)
    give_half.start()
    with jax.named_scope("half"):
        give_half.wait_recv()
    both = rows_ref[core].astype(jnp.float32) + heard[0].astype(jnp.float32)
    chip_ref[0] = both.astype(jnp.bfloat16)
    everywhere(lambda i: pl.when(lower(is_up(i)))(lambda: rows_out(i).start()))

    @pl.when(is_up(1))
    def _():
        with jax.named_scope("next"):
            pl.semaphore_wait(allow.at[0], 1)
        send_z(1, range(2))

    with jax.named_scope("allow"):
        allowed(2, rep_ups)
        allowed(3, ups)
    def body(i, carry):
        for j in range(3):
            pl.when(i == j)(lambda: by_role(j))

        @pl.when(i == 0)
        def _():
            with jax.named_scope("pivots"):
                swap.wait_recv()
                arrive(block_rows, o_recv.at[0])
            with jax.named_scope("scaled"):
                prepare()

        with jax.named_scope("cmp"):
            compare(lax.select(jnp.logical_and(lower(edge), i > 0), 3 - i, i) if chips == 4 and SWAP else i)
        return carry

    lax.fori_loop(0, 3, body, 0)
    by_role(3)
    with jax.named_scope("drain"):
        relayed = sum(len(hops) for hops in relays.values()) * piece

        def total(role):
            rows = (3 if role == RING else 2) * part + 3 * block_rows + 3 * len(direct) * part
            for mode in MODES[role]:
                rows += relayed if mode == RELAY else len(diagonal) * part if mode == ROUTED else 0
            if role != RING:
                rows += (sum(extra(role)) + widens(role)) * len(diagonal) * part
            return rows + (2 * part if role in (LOW_MID, HIGH_MID) else 0)

        if chips != 4:
            gone(total(RING))
        else:
            for role in range(chips):
                pl.when(is_role[role])(lambda: gone(total(role)))
        spot = heard.at[pl.ds(0, chips + 1)]
        remote(spot, spot, out_sem.at[1], p_recv.at[1], partner).wait_send()


def solution(mesh):
    n_vec, n_rep = mesh.shape["vec"], mesh.shape["rep"]
    n_b = 2 if n_rep % 2 == 0 else 1
    n_a = n_rep // n_b
    assert n_vec % 2 == 0 and n_vec > 2 * HALF

    def step(vectors, pivot_index):
        rows, fields = vectors.shape
        count = pivot_index.shape[1]
        dma = pltpu.SemaphoreType.DMA
        vmem = pl.BlockSpec(memory_space=pltpu.VMEM)
        hbm = pl.BlockSpec(memory_space=pltpu.HBM)
        held, win, scaled = pl.pallas_call(
            functools.partial(kernel, n_vec, n_a, n_b),
            out_shape=(
                pltpu.VMEM((2 * HALF + 1, count, rows, rows), jnp.bfloat16),
                pltpu.VMEM((7, rows, fields), jnp.bfloat16),
                pltpu.VMEM((count * rows, fields), jnp.bfloat16),
            ),
            in_specs=[hbm, hbm],
            out_specs=(vmem, vmem, vmem),
            scratch_shapes=[
                pltpu.VMEM((1, count), jnp.int32),
                pltpu.VMEM((2, count, fields // 2), jnp.bfloat16),
                pltpu.VMEM((2, count, fields // 2), jnp.bfloat16),
                pltpu.VMEM((n_vec // 2 + 1, count, fields // 2), jnp.bfloat16),
                dma((2,)), dma((2, 3)), dma((3,)), dma((3, 2)), dma((3,)), dma((3,)), dma((2,)),
                dma((1,)), dma((2,)), pltpu.SemaphoreType.REGULAR((4,)),
            ],
            compiler_params=pltpu.CompilerParams(
                collective_id=0, has_side_effects=True, vmem_limit_bytes=60_800_000
            ),
        )(vectors, pivot_index)
        return pl.pallas_call(
            functools.partial(closing, n_vec),
            out_shape=jax.ShapeDtypeStruct(held.shape, held.dtype),
            in_specs=[vmem, vmem, vmem],
            out_specs=pl.BlockSpec(memory_space=pl.ANY),
            scratch_shapes=[pltpu.VMEM((2, *held.shape[1:]), held.dtype), dma((2 * HALF + 3, CHUNKS))],
            compiler_params=pltpu.CompilerParams(vmem_limit_bytes=24 * 2**20),
        )(held, win, scaled)

    return jax.shard_map(
        step, mesh=mesh, in_specs=(P("vec", None), P("rep", None)),
        out_specs=P(None, "rep", "vec", None), check_vma=False,
    )
```

```python
import functools
import math

import jax
import jax.numpy as jnp
from jax import lax
from jax.experimental import pallas as pl
from jax.experimental.pallas import tpu as pltpu
from jax.sharding import PartitionSpec as P

HALF = 3
NEAR, OUTER, FAR = 0, 1, 2
AT = (3, 5, 2)
LAST = FAR
RELAY, ROUTED, WIDE = range(3)
LOW_END, LOW_MID, HIGH_MID, HIGH_END, RING = range(5)
ACROSS = (HIGH_END, HIGH_MID, LOW_MID, LOW_END)
BESIDE = (LOW_MID, LOW_END, HIGH_END, HIGH_MID)
MODES = (
    (ROUTED, WIDE, WIDE),
    (WIDE, WIDE, ROUTED),
    (ROUTED, WIDE, ROUTED),
    (ROUTED, WIDE, ROUTED),
    (RELAY, RELAY, RELAY),
)


def words(*parts):
    return " ".join(parts)


STEPS = (
    (
        words("z00 up z01 inward", "outward corner z10 z11", "z20 z21 d00 d01", "rows r0"),
        words("d10 d11 r1 h0"),
        words("h1"),
        words("d20 d21 r2"),
    ),
    (
        words("up z00 z10 z11", "z01 d00 rows d01", "corner r0 z20 z21", "r1 d10 d11"),
        words("h1"),
        words("h0"),
        words("d20 d21 r2"),
    ),
    (
        words("up inward z00 z10", "z11 z01 corner d00", "rows d01 z20 z21", "r1 d10 d11 r0"),
        words("h1"),
        words("h0"),
        words("d20 d21 r2"),
    ),
    (
        words("up z00 outward0 z01", "inward corner z10 outward1", "z11 z20 z21 d00", "d01 rows r0"),
        words("d10 d11 r1 h0"),
        words("h1"),
        words("d20 d21 r2"),
    ),
    (
        words("z00 z10 z01 z11", "up d00 d01 corner", "rows z20 z21 d10", "d11 r0 d20 d21", "r1"),
        words("h0"),
        words("h1"),
        words("r2"),
    ),
)
CHUNKS = 1
SWAP = True
SIDES = (-1, 1)


def contract(left, right):
    return lax.dot_general(
        left, right, (((1,), (1,)), ((), ())), preferred_element_type=jnp.float32
    )


def inward(chip, chips):
    return 1 - 2 * (2 * chip // chips) if chips == 4 else 1 + 0 * chip


def pairs(i, core, way):
    if isinstance(i, int) and i == 3 and LAST == FAR:
        return 1, HALF + 1 - 2 * core, 2 * HALF * core
    if isinstance(i, int) and i == 3:
        return 5, HALF - 2 * way, HALF - 2 * way + 1 - 2 * core
    if LAST == FAR:
        step = way * (i % 2) - way * (i // 2)
        mine = HALF + 2 * step
        return (i > 0) + 2 * i, mine, mine + 1 - 2 * core
    near, far = i % 2, i // 2
    mine = HALF + 2 * way * near + far * (1 - 2 * core)
    other = (HALF + 2 * way * near + 1 - 2 * core) * (1 - far) + 2 * HALF * core * far
    return 3 * near + far, mine, other


def products(scaled, right, count):
    value = (contract(scaled, right) * (1.0 / math.sqrt(scaled.shape[1]))).astype(jnp.bfloat16)
    return value.reshape(count, scaled.shape[0] // count, right.shape[0])


def closing(n_vec, held, win, scaled, out_ref, last, sems):
    window, count, block_rows, fields = held.shape[0], held.shape[1], held.shape[2], win.shape[2]
    me = lax.axis_index("vec")
    base, first, second = pairs(3, me % 2, inward(me // 2, n_vec // 2))
    fresh = [second] if LAST == FAR else [first, second]

    def ready(i):
        return pltpu.make_async_copy(held.at[i], out_ref.at[i], sems.at[i, 0])

    some = count // CHUNKS

    def late(j, n):
        ks = pl.ds(n * some, some)
        return pltpu.make_async_copy(last.at[j, ks], out_ref.at[fresh[j], ks], sems.at[window + j, n])

    def others(action):
        for i in range(window):
            unlike = fresh[0] != i
            for spot in fresh[1:]:
                unlike = jnp.logical_and(unlike, spot != i)
            pl.when(unlike)(lambda i=i: action(i))

    with jax.named_scope("s"):
        others(lambda i: ready(i).start())
    right = win[base:base + 2].reshape(2 * block_rows, fields)
    for n in range(CHUNKS):
        with jax.named_scope(f"c{n}"):
            value = products(scaled[n * some * block_rows:(n + 1) * some * block_rows], right, some)
            for j in range(len(fresh)):
                h = 2 - len(fresh) + j
                last[j, n * some:(n + 1) * some] = value[:, :, h * block_rows:(h + 1) * block_rows]
                late(j, n).start()
    with jax.named_scope("w0"):
        others(lambda i: ready(i).wait())
    with jax.named_scope("w1"):
        for j in range(len(fresh)):
            for n in range(CHUNKS):
                late(j, n).wait()


def kernel(
    n_vec, n_a, n_b, vec_ref, index_ref, out_ref, win, scaled, wanted_ref, rows_ref, chip_ref, heard,
    out_sem, z_recv, f_recv, d_recv, r_recv, p_recv, h_recv, o_recv, local_sem, allow,
):
    block_rows, fields = vec_ref.shape
    count = index_ref.shape[1]
    n_rep = n_a * n_b
    chips = n_vec // 2
    part = block_rows // n_rep
    piece = part // 2
    me = lax.axis_index("vec")
    rep = lax.axis_index("rep")
    a, b = rep // n_b, rep % n_b
    chip, core = me // 2, me % 2
    partner = {"vec": me + 1 - 2 * core}
    way = inward(chip, chips)
    short = n_vec <= 16

    def chip_index(offset):
        return (chip + offset + chips) % chips

    def at_chip(offset, which):
        return {"vec": 2 * chip_index(offset) + which}

    def rep_of(da, db):
        return ((a + da + n_a) % n_a) * n_b + (b + db + n_b) % n_b

    direct = [(0, i) for i in range(1, n_b)] + [(i, 0) for i in range(1, n_a)]
    diagonal = [(i, j) for i in range(1, n_a) for j in range(1, n_b)]
    relays = {}
    for t, (da, db) in enumerate(direct):
        if da == 0:
            relays[t] = [((i, 0), diagonal.index((i, db))) for i in range(1, n_a)]
        else:
            relays[t] = [((0, j), diagonal.index((da, j))) for j in range(1, n_b)]
    side = [0 if da == 0 else 1 for da, _ in direct]

    own_copy = pltpu.make_async_copy(vec_ref, win.at[0], local_sem.at[0])
    index_copy = pltpu.make_async_copy(index_ref, wanted_ref, local_sem.at[1])
    own_copy.start()
    index_copy.start()

    def is_up(offset):
        return chip_index(offset) > chip

    def rep_is_up(da, db):
        return rep_of(da, db) > rep

    def number_of(flags):
        return sum((flag.astype(jnp.int32) for flag in flags), jnp.int32(0))

    def everywhere(action):
        def body(i, carry):
            action(i)
            return carry

        lax.fori_loop(1, chips, body, 0, unroll=short)

    barrier = pltpu.get_barrier_semaphore()
    lower = jnp.logical_not

    def meet(sem, when, device):
        pl.when(when)(lambda: pl.semaphore_signal(sem, inc=1, device_id=device))

    def allowed(i, times):
        pl.when(times > 0)(lambda: pl.semaphore_wait(allow.at[i], times))

    sides = (1, -1)
    everywhere(lambda i: meet(barrier, is_up(i), at_chip(i, core)))
    opposite = (1,) if chips == 4 else sides
    for step in opposite:
        meet(barrier, is_up(step), at_chip(step, 1 - core))
    for hop in direct:
        meet(barrier, rep_is_up(*hop), {"rep": rep_of(*hop)})
    pl.semaphore_signal(barrier, inc=1, device_id=partner)
    ups = number_of([is_up(step) for step in opposite])
    downs = number_of([chip > 0]) if chips == 4 else 2 - ups
    rep_ups = number_of([rep_is_up(*hop) for hop in direct])
    with jax.named_scope("barrier"):
        pl.semaphore_wait(barrier, chip + downs + (len(direct) - rep_ups) + 1)
    meet(allow.at[0], lower(is_up(-1)), at_chip(-1, core))
    everywhere(lambda i: meet(allow.at[1], lower(is_up(i)), at_chip(i, core)))
    for hop in direct:
        meet(allow.at[2], lower(rep_is_up(*hop)), {"rep": rep_of(*hop)})
    if chips == 4:
        meet(allow.at[3], chip > 0, at_chip(-1, 1 - core))
    else:
        for step in sides:
            meet(allow.at[3], lower(is_up(step)), at_chip(step, 1 - core))

    def remote(src, dst, send_sem, recv_sem, device):
        return pltpu.make_async_remote_copy(
            src_ref=src, dst_ref=dst, send_sem=send_sem, recv_sem=recv_sem, device_id=device
        )

    def arrive(rows, sem):
        spot = scaled.at[pl.ds(0, rows)]
        remote(spot, spot, out_sem.at[0], sem, partner).wait_recv()

    def gone(rows):
        spot = scaled.at[pl.ds(0, rows)]
        remote(spot, spot, out_sem.at[0], o_recv.at[0], partner).wait_send()

    def rows_at(which, h):
        return pl.ds(pl.multiple_of(which * part + h * piece, piece), piece)

    def quarter(da, db, h):
        return rows_at(rep_of(-da, -db), h)

    own = [rows_at(rep, h) for h in range(2)]

    if chips == 4:
        edge = jnp.logical_or(chip == 0, chip == chips - 1)
    else:
        edge = chip < 0

    def z_copy(step, which):
        looks = inward(chip_index(step), chips)
        slot = (1 + step * looks) // 2
        if which < 2:
            rows = own[which]
        else:
            rows = pl.ds(pl.multiple_of(rep_of(*diagonal[which - 2]) * part, part), part)
        return remote(
            vec_ref.at[rows], win.at[AT[NEAR] + (AT[OUTER] - AT[NEAR]) * slot, rows],
            out_sem.at[0], z_recv.at[slot, jnp.minimum(which, 2)], at_chip(step, core),
        )

    def passes(slot):
        return lower(edge) if chips == 4 else core == slot

    def pass_on(slot, h):
        step = -way if slot == NEAR else way
        return remote(
            win.at[AT[slot], own[h]], win.at[AT[FAR], own[h]], out_sem.at[0], f_recv.at[h],
            at_chip(step, 1 - core),
        )

    def d_copy(slot, t, h):
        spot = win.at[AT[slot], own[h]]
        return remote(spot, spot, out_sem.at[0], d_recv.at[slot, h], {"rep": rep_of(*direct[t])})

    def routed_copy(slot, number, h):
        spot = win.at[AT[slot], own[h]]
        return remote(spot, spot, out_sem.at[0], r_recv.at[slot], {"rep": rep_of(*diagonal[number])})

    def r_copy(slot, t, hop):
        spot = win.at[AT[slot], quarter(*direct[t], side[t])]
        return remote(spot, spot, out_sem.at[0], r_recv.at[slot], {"rep": rep_of(*hop)})

    def hand(slot, rows):
        if slot != FAR:
            remote(
                win.at[AT[slot], rows], win.at[AT[slot] + 1, rows], out_sem.at[0], h_recv.at[slot], partner
            ).start()

    def handed(slot):
        arrive(block_rows, h_recv.at[slot])

    half = fields // 2

    def halves(src, dst, k, device):
        return remote(src, heard.at[dst], out_sem.at[1], p_recv.at[k], device)

    give_half = halves(rows_ref.at[1 - core], 0, 0, partner)
    swap = halves(chip_ref.at[1], chips, 2, partner)

    def rows_out(i):
        return halves(chip_ref.at[0], i, 1, at_chip(i, core))

    def first(slot, h, mode):
        arrive(piece, f_recv.at[h] if slot == FAR else z_recv.at[slot, h])
        if slot != FAR:
            pl.when(passes(slot))(lambda: pass_on(slot, h).start())
        if mode == ROUTED and slot != NEAR:
            for number in range(len(diagonal)):
                routed_copy(slot, number, h).start()
        for t in range(len(direct)):
            d_copy(slot, t, h).start()
        hand(slot, own[h])

    def second(slot, h, mode):
        if direct:
            arrive(len(direct) * piece, d_recv.at[slot, h])
        for t in range(len(direct)):
            if side[t] == h and mode == RELAY:
                for hop, number in relays[t]:
                    r_copy(slot, t, hop).start()
            hand(slot, quarter(*direct[t], h))

    def third(slot, mode, role):
        if diagonal:
            if mode != WIDE:
                sem = r_recv.at[slot]
            else:
                sem = f_recv.at[2] if slot == FAR else z_recv.at[slot, 2]
            arrive(len(diagonal) * part, sem)
        if slot == NEAR and widens(role):
            for spot in diagonal:
                rows = pl.ds(pl.multiple_of(rep_of(*spot) * part, part), part)
                remote(
                    win.at[AT[NEAR], rows], win.at[AT[FAR], rows], out_sem.at[0], f_recv.at[2],
                    at_chip(-way, 1 - core),
                ).start()
        for spot in diagonal:
            for h in range(2):
                hand(slot, quarter(*spot, h))

    partner_own = remote(vec_ref, win.at[1], out_sem.at[0], o_recv.at[0], partner)

    def prepare():
        mine, other = chip_ref[1].astype(jnp.float32), heard[chips].astype(jnp.float32)
        pivots = jnp.concatenate(
            [jnp.where(core == 0, mine, other), jnp.where(core == 0, other, mine)], axis=1
        )
        level = jnp.sum(pivots, axis=1, keepdims=True) / fields
        pivots = pivots - level
        block = win[0].astype(jnp.float32)
        for k in range(count):
            scaled[k * block_rows:(k + 1) * block_rows, :] = (block * pivots[k:k + 1, :]).astype(jnp.bfloat16)

    def compare(i):
        base, mine_at, other_at = pairs(i, core, way)
        value = products(scaled[...], win[pl.ds(base, 2)].reshape(2 * block_rows, fields), count)
        out_ref[mine_at] = value[:, :, :block_rows]
        out_ref[other_at] = value[:, :, block_rows:]

    def send_z(step, steps):
        for which in steps:
            z_copy(step, which).start()

    def send_wide(step):
        if diagonal:
            send_z(step, range(2, 2 + len(diagonal)))

    def extra(role):
        ends = role in (LOW_END, HIGH_END)
        inside = MODES[BESIDE[role]][OUTER] if ends else MODES[ACROSS[role]][NEAR]
        outside = MODES[ACROSS[role]][OUTER] if ends else MODES[BESIDE[role]][NEAR]
        return inside == WIDE, outside == WIDE

    def widens(role):
        return role in (LOW_MID, HIGH_MID) and MODES[BESIDE[role]][FAR] == WIDE

    def up():
        allowed(1, chips - 1 - chip)
        pl.when(is_up(-1))(lambda: send_z(-1, range(2)))
        everywhere(lambda i: pl.when(is_up(i))(lambda: rows_out(i).start()))

    def add_rows():
        spot = heard.at[pl.ds(1, chips - 1)]
        remote(spot, spot, out_sem.at[1], p_recv.at[1], partner).wait_recv()
        total = lax.fori_loop(
            1, chips, lambda i, total: total + heard[i].astype(jnp.float32),
            chip_ref[0].astype(jnp.float32), unroll=short,
        )
        chip_ref[1] = total.astype(jnp.bfloat16)
        swap.start()

    def run(steps, role):
        for name in steps.split():
            slot = int(name[1]) if name[1].isdigit() else None
            with jax.named_scope(name):
                if name == "up":
                    up()
                elif name in ("inward", "outward", "outward0", "outward1"):
                    if extra(role)[name != "inward"]:
                        for step in sides:
                            when = (way == step) == (name == "inward")
                            if name[-1].isdigit():
                                when = jnp.logical_and(when, core == int(name[-1]))
                            pl.when(when)(lambda: send_wide(step))
                elif name == "corner":
                    if direct:
                        pl.semaphore_wait(allow.at[4], len(direct))
                    if MODES[role][NEAR] == ROUTED:
                        for h in range(2):
                            for number in range(len(diagonal)):
                                routed_copy(NEAR, number, h).start()
                elif name == "rows":
                    add_rows()
                elif name[0] == "z":
                    first(slot, int(name[2]), MODES[role][slot])
                elif name[0] == "d":
                    second(slot, int(name[2]), MODES[role][slot])
                elif name[0] == "r":
                    third(slot, MODES[role][slot], role)
                else:
                    handed(slot)

    is_role = [chip == 0, chip == 1, chip == 2, chip == 3]

    def by_role(i):
        if chips != 4:
            run(STEPS[RING][i], RING)
            return
        for role in range(chips):
            pl.when(is_role[role])(lambda: run(STEPS[role][i], role))

    for h in range(2):
        for step in SIDES:
            pl.when(lower(is_up(step)))(lambda: z_copy(step, h).start())
    partner_own.start()

    index_copy.wait()
    own_copy.wait()
    wanted = wanted_ref[...] - me * block_rows
    spots = lax.broadcasted_iota(jnp.int32, (block_rows, count), 0)
    onehot = (spots == wanted).astype(jnp.bfloat16)
    mine = lax.dot_general(
        onehot, win[0], (((0,), (0,)), ((), ())), preferred_element_type=jnp.float32
    )
    rows_ref[0] = mine[:, :half].astype(jnp.bfloat16)
    rows_ref[1] = mine[:, half:].astype(jnp.bfloat16)
    give_half.start()
    with jax.named_scope("half"):
        give_half.wait_recv()
    both = rows_ref[core].astype(jnp.float32) + heard[0].astype(jnp.float32)
    chip_ref[0] = both.astype(jnp.bfloat16)
    everywhere(lambda i: pl.when(lower(is_up(i)))(lambda: rows_out(i).start()))

    @pl.when(is_up(1))
    def _():
        with jax.named_scope("next"):
            pl.semaphore_wait(allow.at[0], 1)
        send_z(1, range(2))

    with jax.named_scope("allow"):
        allowed(2, rep_ups)
        allowed(3, ups)
        for hop in direct:
            pl.semaphore_signal(allow.at[4], inc=1, device_id={"rep": rep_of(*hop)})
    def body(i, carry):
        for j in range(3):
            pl.when(i == j)(lambda: by_role(j))

        @pl.when(i == 0)
        def _():
            with jax.named_scope("pivots"):
                swap.wait_recv()
                arrive(block_rows, o_recv.at[0])
            with jax.named_scope("scaled"):
                prepare()

        with jax.named_scope("cmp"):
            compare(lax.select(jnp.logical_and(lower(edge), i > 0), 3 - i, i) if chips == 4 and SWAP else i)
        return carry

    lax.fori_loop(0, 3, body, 0)
    by_role(3)
    with jax.named_scope("drain"):
        relayed = sum(len(hops) for hops in relays.values()) * piece

        def total(role):
            rows = (3 if role == RING else 2) * part + 3 * block_rows + 3 * len(direct) * part
            for mode in MODES[role]:
                rows += relayed if mode == RELAY else len(diagonal) * part if mode == ROUTED else 0
            if role != RING:
                rows += (sum(extra(role)) + widens(role)) * len(diagonal) * part
            return rows + (2 * part if role in (LOW_MID, HIGH_MID) else 0)

        if chips != 4:
            gone(total(RING))
        else:
            for role in range(chips):
                pl.when(is_role[role])(lambda: gone(total(role)))
        spot = heard.at[pl.ds(0, chips + 1)]
        remote(spot, spot, out_sem.at[1], p_recv.at[1], partner).wait_send()


def solution(mesh):
    n_vec, n_rep = mesh.shape["vec"], mesh.shape["rep"]
    n_b = 2 if n_rep % 2 == 0 else 1
    n_a = n_rep // n_b
    assert n_vec % 2 == 0 and n_vec > 2 * HALF

    def step(vectors, pivot_index):
        rows, fields = vectors.shape
        count = pivot_index.shape[1]
        dma = pltpu.SemaphoreType.DMA
        vmem = pl.BlockSpec(memory_space=pltpu.VMEM)
        hbm = pl.BlockSpec(memory_space=pltpu.HBM)
        held, win, scaled = pl.pallas_call(
            functools.partial(kernel, n_vec, n_a, n_b),
            out_shape=(
                pltpu.VMEM((2 * HALF + 1, count, rows, rows), jnp.bfloat16),
                pltpu.VMEM((7, rows, fields), jnp.bfloat16),
                pltpu.VMEM((count * rows, fields), jnp.bfloat16),
            ),
            in_specs=[hbm, hbm],
            out_specs=(vmem, vmem, vmem),
            scratch_shapes=[
                pltpu.VMEM((1, count), jnp.int32),
                pltpu.VMEM((2, count, fields // 2), jnp.bfloat16),
                pltpu.VMEM((2, count, fields // 2), jnp.bfloat16),
                pltpu.VMEM((n_vec // 2 + 1, count, fields // 2), jnp.bfloat16),
                dma((2,)), dma((2, 3)), dma((3,)), dma((3, 2)), dma((3,)), dma((3,)), dma((2,)),
                dma((1,)), dma((2,)), pltpu.SemaphoreType.REGULAR((5,)),
            ],
            compiler_params=pltpu.CompilerParams(
                collective_id=0, has_side_effects=True, vmem_limit_bytes=60_800_000
            ),
        )(vectors, pivot_index)
        return pl.pallas_call(
            functools.partial(closing, n_vec),
            out_shape=jax.ShapeDtypeStruct(held.shape, held.dtype),
            in_specs=[vmem, vmem, vmem],
            out_specs=pl.BlockSpec(memory_space=pl.ANY),
            scratch_shapes=[pltpu.VMEM((2, *held.shape[1:]), held.dtype), dma((2 * HALF + 3, CHUNKS))],
            compiler_params=pltpu.CompilerParams(vmem_limit_bytes=24 * 2**20),
        )(held, win, scaled)

    return jax.shard_map(
        step, mesh=mesh, in_specs=(P("vec", None), P("rep", None)),
        out_specs=P(None, "rep", "vec", None), check_vma=False,
    )
```

```python
import functools
import math

import jax
import jax.numpy as jnp
from jax import lax
from jax.experimental import pallas as pl
from jax.experimental.pallas import tpu as pltpu
from jax.sharding import PartitionSpec as P

HALF = 3
NEAR, OUTER, FAR = 0, 1, 2
AT = (3, 5, 2)
LAST = FAR
RELAY, ROUTED, WIDE = range(3)
LOW_END, LOW_MID, HIGH_MID, HIGH_END, RING = range(5)
ACROSS = (HIGH_END, HIGH_MID, LOW_MID, LOW_END)
BESIDE = (LOW_MID, LOW_END, HIGH_END, HIGH_MID)
MODES = (
    (ROUTED, WIDE, WIDE),
    (WIDE, WIDE, ROUTED),
    (ROUTED, WIDE, ROUTED),
    (ROUTED, WIDE, ROUTED),
    (RELAY, RELAY, RELAY),
)


def words(*parts):
    return " ".join(parts)


STEPS = (
    (
        words("up z00 z01 inward", "outward corner z10 z11", "z20 rows z21"),
        words("d00 d01 r0 d10", "d11 r1 h0"),
        words("h1"),
        words("d20 d21 r2"),
    ),
    (
        words("up z00 z10 z11", "z01 d00 rows d01", "corner r0 z20 z21", "r1 d10 d11"),
        words("h1"),
        words("h0"),
        words("d20 d21 r2"),
    ),
    (
        words("up inward z00 z10", "z11 z01 corner d00", "rows d01 z20 z21", "r1 d10 d11"),
        words("r0 h1"),
        words("h0"),
        words("d20 d21 r2"),
    ),
    (
        words("up z00 outward0 z01", "inward corner z10 outward1", "z11 z20 rows z21", "d00 d01"),
        words("r0 d10 d11 r1", "h0"),
        words("h1"),
        words("d20 d21 r2"),
    ),
    (
        words("z00 z10 z01 z11", "up d00 d01 corner", "rows z20 z21 d10", "d11 r0 d20 d21", "r1"),
        words("h0"),
        words("h1"),
        words("r2"),
    ),
)
CHUNKS = 1
SWAP = True
SIDES = (-1, 1)


def contract(left, right):
    return lax.dot_general(
        left, right, (((1,), (1,)), ((), ())), preferred_element_type=jnp.float32
    )


def inward(chip, chips):
    return 1 - 2 * (2 * chip // chips) if chips == 4 else 1 + 0 * chip


def pairs(i, core, way):
    if isinstance(i, int) and i == 3 and LAST == FAR:
        return 1, HALF + 1 - 2 * core, 2 * HALF * core
    if isinstance(i, int) and i == 3:
        return 5, HALF - 2 * way, HALF - 2 * way + 1 - 2 * core
    if LAST == FAR:
        step = way * (i % 2) - way * (i // 2)
        mine = HALF + 2 * step
        return (i > 0) + 2 * i, mine, mine + 1 - 2 * core
    near, far = i % 2, i // 2
    mine = HALF + 2 * way * near + far * (1 - 2 * core)
    other = (HALF + 2 * way * near + 1 - 2 * core) * (1 - far) + 2 * HALF * core * far
    return 3 * near + far, mine, other


def products(scaled, right, count):
    value = (contract(scaled, right) * (1.0 / math.sqrt(scaled.shape[1]))).astype(jnp.bfloat16)
    return value.reshape(count, scaled.shape[0] // count, right.shape[0])


def closing(n_vec, held, win, scaled, out_ref, last, sems):
    window, count, block_rows, fields = held.shape[0], held.shape[1], held.shape[2], win.shape[2]
    me = lax.axis_index("vec")
    base, first, second = pairs(3, me % 2, inward(me // 2, n_vec // 2))
    fresh = [second] if LAST == FAR else [first, second]

    def ready(i):
        return pltpu.make_async_copy(held.at[i], out_ref.at[i], sems.at[i, 0])

    some = count // CHUNKS

    def late(j, n):
        ks = pl.ds(n * some, some)
        return pltpu.make_async_copy(last.at[j, ks], out_ref.at[fresh[j], ks], sems.at[window + j, n])

    def others(action):
        for i in range(window):
            unlike = fresh[0] != i
            for spot in fresh[1:]:
                unlike = jnp.logical_and(unlike, spot != i)
            pl.when(unlike)(lambda i=i: action(i))

    with jax.named_scope("s"):
        others(lambda i: ready(i).start())
    right = win[base:base + 2].reshape(2 * block_rows, fields)
    for n in range(CHUNKS):
        with jax.named_scope(f"c{n}"):
            value = products(scaled[n * some * block_rows:(n + 1) * some * block_rows], right, some)
            for j in range(len(fresh)):
                h = 2 - len(fresh) + j
                last[j, n * some:(n + 1) * some] = value[:, :, h * block_rows:(h + 1) * block_rows]
                late(j, n).start()
    with jax.named_scope("w0"):
        others(lambda i: ready(i).wait())
    with jax.named_scope("w1"):
        for j in range(len(fresh)):
            for n in range(CHUNKS):
                late(j, n).wait()


def kernel(
    n_vec, n_a, n_b, vec_ref, index_ref, out_ref, win, scaled, wanted_ref, rows_ref, chip_ref, heard,
    out_sem, z_recv, f_recv, d_recv, r_recv, p_recv, h_recv, o_recv, local_sem, allow,
):
    block_rows, fields = vec_ref.shape
    count = index_ref.shape[1]
    n_rep = n_a * n_b
    chips = n_vec // 2
    part = block_rows // n_rep
    piece = part // 2
    me = lax.axis_index("vec")
    rep = lax.axis_index("rep")
    a, b = rep // n_b, rep % n_b
    chip, core = me // 2, me % 2
    partner = {"vec": me + 1 - 2 * core}
    way = inward(chip, chips)
    short = n_vec <= 16

    def chip_index(offset):
        return (chip + offset + chips) % chips

    def at_chip(offset, which):
        return {"vec": 2 * chip_index(offset) + which}

    def rep_of(da, db):
        return ((a + da + n_a) % n_a) * n_b + (b + db + n_b) % n_b

    direct = [(0, i) for i in range(1, n_b)] + [(i, 0) for i in range(1, n_a)]
    diagonal = [(i, j) for i in range(1, n_a) for j in range(1, n_b)]
    relays = {}
    for t, (da, db) in enumerate(direct):
        if da == 0:
            relays[t] = [((i, 0), diagonal.index((i, db))) for i in range(1, n_a)]
        else:
            relays[t] = [((0, j), diagonal.index((da, j))) for j in range(1, n_b)]
    side = [0 if da == 0 else 1 for da, _ in direct]

    own_copy = pltpu.make_async_copy(vec_ref, win.at[0], local_sem.at[0])
    index_copy = pltpu.make_async_copy(index_ref, wanted_ref, local_sem.at[1])
    own_copy.start()
    index_copy.start()

    def is_up(offset):
        return chip_index(offset) > chip

    def rep_is_up(da, db):
        return rep_of(da, db) > rep

    def number_of(flags):
        return sum((flag.astype(jnp.int32) for flag in flags), jnp.int32(0))

    def everywhere(action):
        def body(i, carry):
            action(i)
            return carry

        lax.fori_loop(1, chips, body, 0, unroll=short)

    barrier = pltpu.get_barrier_semaphore()
    lower = jnp.logical_not

    def meet(sem, when, device):
        pl.when(when)(lambda: pl.semaphore_signal(sem, inc=1, device_id=device))

    def allowed(i, times):
        pl.when(times > 0)(lambda: pl.semaphore_wait(allow.at[i], times))

    sides = (1, -1)
    everywhere(lambda i: meet(barrier, is_up(i), at_chip(i, core)))
    opposite = (1,) if chips == 4 else sides
    for step in opposite:
        meet(barrier, is_up(step), at_chip(step, 1 - core))
    for hop in direct:
        meet(barrier, rep_is_up(*hop), {"rep": rep_of(*hop)})
    pl.semaphore_signal(barrier, inc=1, device_id=partner)
    ups = number_of([is_up(step) for step in opposite])
    downs = number_of([chip > 0]) if chips == 4 else 2 - ups
    rep_ups = number_of([rep_is_up(*hop) for hop in direct])
    with jax.named_scope("barrier"):
        pl.semaphore_wait(barrier, chip + downs + (len(direct) - rep_ups) + 1)
    meet(allow.at[0], lower(is_up(-1)), at_chip(-1, core))
    everywhere(lambda i: meet(allow.at[1], lower(is_up(i)), at_chip(i, core)))
    for hop in direct:
        meet(allow.at[2], lower(rep_is_up(*hop)), {"rep": rep_of(*hop)})
    if chips == 4:
        meet(allow.at[3], chip > 0, at_chip(-1, 1 - core))
    else:
        for step in sides:
            meet(allow.at[3], lower(is_up(step)), at_chip(step, 1 - core))

    def remote(src, dst, send_sem, recv_sem, device):
        return pltpu.make_async_remote_copy(
            src_ref=src, dst_ref=dst, send_sem=send_sem, recv_sem=recv_sem, device_id=device
        )

    def arrive(rows, sem):
        spot = scaled.at[pl.ds(0, rows)]
        remote(spot, spot, out_sem.at[0], sem, partner).wait_recv()

    def gone(rows):
        spot = scaled.at[pl.ds(0, rows)]
        remote(spot, spot, out_sem.at[0], o_recv.at[0], partner).wait_send()

    def rows_at(which, h):
        return pl.ds(pl.multiple_of(which * part + h * piece, piece), piece)

    def quarter(da, db, h):
        return rows_at(rep_of(-da, -db), h)

    own = [rows_at(rep, h) for h in range(2)]

    if chips == 4:
        edge = jnp.logical_or(chip == 0, chip == chips - 1)
    else:
        edge = chip < 0

    def z_copy(step, which):
        looks = inward(chip_index(step), chips)
        slot = (1 + step * looks) // 2
        if which < 2:
            rows = own[which]
        else:
            rows = pl.ds(pl.multiple_of(rep_of(*diagonal[which - 2]) * part, part), part)
        return remote(
            vec_ref.at[rows], win.at[AT[NEAR] + (AT[OUTER] - AT[NEAR]) * slot, rows],
            out_sem.at[0], z_recv.at[slot, jnp.minimum(which, 2)], at_chip(step, core),
        )

    def passes(slot):
        return lower(edge) if chips == 4 else core == slot

    def pass_on(slot, h):
        step = -way if slot == NEAR else way
        return remote(
            win.at[AT[slot], own[h]], win.at[AT[FAR], own[h]], out_sem.at[0], f_recv.at[h],
            at_chip(step, 1 - core),
        )

    def d_copy(slot, t, h):
        spot = win.at[AT[slot], own[h]]
        return remote(spot, spot, out_sem.at[0], d_recv.at[slot, h], {"rep": rep_of(*direct[t])})

    def routed_copy(slot, number, h):
        spot = win.at[AT[slot], own[h]]
        return remote(spot, spot, out_sem.at[0], r_recv.at[slot], {"rep": rep_of(*diagonal[number])})

    def r_copy(slot, t, hop):
        spot = win.at[AT[slot], quarter(*direct[t], side[t])]
        return remote(spot, spot, out_sem.at[0], r_recv.at[slot], {"rep": rep_of(*hop)})

    def hand(slot, rows):
        if slot != FAR:
            remote(
                win.at[AT[slot], rows], win.at[AT[slot] + 1, rows], out_sem.at[0], h_recv.at[slot], partner
            ).start()

    def handed(slot):
        arrive(block_rows, h_recv.at[slot])

    half = fields // 2

    def halves(src, dst, k, device):
        return remote(src, heard.at[dst], out_sem.at[1], p_recv.at[k], device)

    give_half = halves(rows_ref.at[1 - core], 0, 0, partner)
    swap = halves(chip_ref.at[1], chips, 2, partner)

    def rows_out(i):
        return halves(chip_ref.at[0], i, 1, at_chip(i, core))

    def first(slot, h, mode):
        arrive(piece, f_recv.at[h] if slot == FAR else z_recv.at[slot, h])
        if slot != FAR:
            pl.when(passes(slot))(lambda: pass_on(slot, h).start())
        if mode == ROUTED and slot != NEAR:
            for number in range(len(diagonal)):
                routed_copy(slot, number, h).start()
        for t in range(len(direct)):
            d_copy(slot, t, h).start()
        hand(slot, own[h])

    def second(slot, h, mode):
        if direct:
            arrive(len(direct) * piece, d_recv.at[slot, h])
        for t in range(len(direct)):
            if side[t] == h and mode == RELAY:
                for hop, number in relays[t]:
                    r_copy(slot, t, hop).start()
            hand(slot, quarter(*direct[t], h))

    def third(slot, mode, role):
        if diagonal:
            if mode != WIDE:
                sem = r_recv.at[slot]
            else:
                sem = f_recv.at[2] if slot == FAR else z_recv.at[slot, 2]
            arrive(len(diagonal) * part, sem)
        if slot == NEAR and widens(role):
            for spot in diagonal:
                rows = pl.ds(pl.multiple_of(rep_of(*spot) * part, part), part)
                remote(
                    win.at[AT[NEAR], rows], win.at[AT[FAR], rows], out_sem.at[0], f_recv.at[2],
                    at_chip(-way, 1 - core),
                ).start()
        for spot in diagonal:
            for h in range(2):
                hand(slot, quarter(*spot, h))

    partner_own = remote(vec_ref, win.at[1], out_sem.at[0], o_recv.at[0], partner)

    def prepare():
        mine, other = chip_ref[1].astype(jnp.float32), heard[chips].astype(jnp.float32)
        pivots = jnp.concatenate(
            [jnp.where(core == 0, mine, other), jnp.where(core == 0, other, mine)], axis=1
        )
        level = jnp.sum(pivots, axis=1, keepdims=True) / fields
        pivots = pivots - level
        block = win[0].astype(jnp.float32)
        for k in range(count):
            scaled[k * block_rows:(k + 1) * block_rows, :] = (block * pivots[k:k + 1, :]).astype(jnp.bfloat16)

    def compare(i):
        base, mine_at, other_at = pairs(i, core, way)
        value = products(scaled[...], win[pl.ds(base, 2)].reshape(2 * block_rows, fields), count)
        out_ref[mine_at] = value[:, :, :block_rows]
        out_ref[other_at] = value[:, :, block_rows:]

    def send_z(step, steps):
        for which in steps:
            z_copy(step, which).start()

    def send_wide(step):
        if diagonal:
            send_z(step, range(2, 2 + len(diagonal)))

    def extra(role):
        ends = role in (LOW_END, HIGH_END)
        inside = MODES[BESIDE[role]][OUTER] if ends else MODES[ACROSS[role]][NEAR]
        outside = MODES[ACROSS[role]][OUTER] if ends else MODES[BESIDE[role]][NEAR]
        return inside == WIDE, outside == WIDE

    def widens(role):
        return role in (LOW_MID, HIGH_MID) and MODES[BESIDE[role]][FAR] == WIDE

    def up():
        allowed(1, chips - 1 - chip)
        pl.when(is_up(-1))(lambda: send_z(-1, range(2)))
        everywhere(lambda i: pl.when(is_up(i))(lambda: rows_out(i).start()))

    def add_rows():
        spot = heard.at[pl.ds(1, chips - 1)]
        remote(spot, spot, out_sem.at[1], p_recv.at[1], partner).wait_recv()
        total = lax.fori_loop(
            1, chips, lambda i, total: total + heard[i].astype(jnp.float32),
            chip_ref[0].astype(jnp.float32), unroll=short,
        )
        chip_ref[1] = total.astype(jnp.bfloat16)
        swap.start()

    def run(steps, role):
        for name in steps.split():
            slot = int(name[1]) if name[1].isdigit() else None
            with jax.named_scope(name):
                if name == "up":
                    up()
                elif name in ("inward", "outward", "outward0", "outward1"):
                    if extra(role)[name != "inward"]:
                        for step in sides:
                            when = (way == step) == (name == "inward")
                            if name[-1].isdigit():
                                when = jnp.logical_and(when, core == int(name[-1]))
                            pl.when(when)(lambda: send_wide(step))
                elif name == "corner":
                    if direct:
                        pl.semaphore_wait(allow.at[4], len(direct))
                    if MODES[role][NEAR] == ROUTED:
                        for h in range(2):
                            for number in range(len(diagonal)):
                                routed_copy(NEAR, number, h).start()
                elif name == "rows":
                    add_rows()
                elif name[0] == "z":
                    first(slot, int(name[2]), MODES[role][slot])
                elif name[0] == "d":
                    second(slot, int(name[2]), MODES[role][slot])
                elif name[0] == "r":
                    third(slot, MODES[role][slot], role)
                else:
                    handed(slot)

    is_role = [chip == 0, chip == 1, chip == 2, chip == 3]

    def by_role(i):
        if chips != 4:
            run(STEPS[RING][i], RING)
            return
        for role in range(chips):
            pl.when(is_role[role])(lambda: run(STEPS[role][i], role))

    for h in range(2):
        for step in SIDES:
            pl.when(lower(is_up(step)))(lambda: z_copy(step, h).start())
    partner_own.start()

    index_copy.wait()
    own_copy.wait()
    wanted = wanted_ref[...] - me * block_rows
    spots = lax.broadcasted_iota(jnp.int32, (block_rows, count), 0)
    onehot = (spots == wanted).astype(jnp.bfloat16)
    mine = lax.dot_general(
        onehot, win[0], (((0,), (0,)), ((), ())), preferred_element_type=jnp.float32
    )
    rows_ref[0] = mine[:, :half].astype(jnp.bfloat16)
    rows_ref[1] = mine[:, half:].astype(jnp.bfloat16)
    give_half.start()
    with jax.named_scope("half"):
        give_half.wait_recv()
    both = rows_ref[core].astype(jnp.float32) + heard[0].astype(jnp.float32)
    chip_ref[0] = both.astype(jnp.bfloat16)
    everywhere(lambda i: pl.when(lower(is_up(i)))(lambda: rows_out(i).start()))

    @pl.when(is_up(1))
    def _():
        with jax.named_scope("next"):
            pl.semaphore_wait(allow.at[0], 1)
        send_z(1, range(2))

    with jax.named_scope("allow"):
        allowed(2, rep_ups)
        allowed(3, ups)
        for hop in direct:
            pl.semaphore_signal(allow.at[4], inc=1, device_id={"rep": rep_of(*hop)})
    def body(i, carry):
        for j in range(3):
            pl.when(i == j)(lambda: by_role(j))

        @pl.when(i == 0)
        def _():
            with jax.named_scope("pivots"):
                swap.wait_recv()
                arrive(block_rows, o_recv.at[0])
            with jax.named_scope("scaled"):
                prepare()

        with jax.named_scope("cmp"):
            compare(lax.select(jnp.logical_and(lower(edge), i > 0), 3 - i, i) if chips == 4 and SWAP else i)
        return carry

    lax.fori_loop(0, 3, body, 0)
    by_role(3)
    with jax.named_scope("drain"):
        relayed = sum(len(hops) for hops in relays.values()) * piece

        def total(role):
            rows = (3 if role == RING else 2) * part + 3 * block_rows + 3 * len(direct) * part
            for mode in MODES[role]:
                rows += relayed if mode == RELAY else len(diagonal) * part if mode == ROUTED else 0
            if role != RING:
                rows += (sum(extra(role)) + widens(role)) * len(diagonal) * part
            return rows + (2 * part if role in (LOW_MID, HIGH_MID) else 0)

        if chips != 4:
            gone(total(RING))
        else:
            for role in range(chips):
                pl.when(is_role[role])(lambda: gone(total(role)))
        spot = heard.at[pl.ds(0, chips + 1)]
        remote(spot, spot, out_sem.at[1], p_recv.at[1], partner).wait_send()


def solution(mesh):
    n_vec, n_rep = mesh.shape["vec"], mesh.shape["rep"]
    n_b = 2 if n_rep % 2 == 0 else 1
    n_a = n_rep // n_b
    assert n_vec % 2 == 0 and n_vec > 2 * HALF

    def step(vectors, pivot_index):
        rows, fields = vectors.shape
        count = pivot_index.shape[1]
        dma = pltpu.SemaphoreType.DMA
        vmem = pl.BlockSpec(memory_space=pltpu.VMEM)
        hbm = pl.BlockSpec(memory_space=pltpu.HBM)
        held, win, scaled = pl.pallas_call(
            functools.partial(kernel, n_vec, n_a, n_b),
            out_shape=(
                pltpu.VMEM((2 * HALF + 1, count, rows, rows), jnp.bfloat16),
                pltpu.VMEM((7, rows, fields), jnp.bfloat16),
                pltpu.VMEM((count * rows, fields), jnp.bfloat16),
            ),
            in_specs=[hbm, hbm],
            out_specs=(vmem, vmem, vmem),
            scratch_shapes=[
                pltpu.VMEM((1, count), jnp.int32),
                pltpu.VMEM((2, count, fields // 2), jnp.bfloat16),
                pltpu.VMEM((2, count, fields // 2), jnp.bfloat16),
                pltpu.VMEM((n_vec // 2 + 1, count, fields // 2), jnp.bfloat16),
                dma((2,)), dma((2, 3)), dma((3,)), dma((3, 2)), dma((3,)), dma((3,)), dma((2,)),
                dma((1,)), dma((2,)), pltpu.SemaphoreType.REGULAR((5,)),
            ],
            compiler_params=pltpu.CompilerParams(
                collective_id=0, has_side_effects=True, vmem_limit_bytes=60_800_000
            ),
        )(vectors, pivot_index)
        return pl.pallas_call(
            functools.partial(closing, n_vec),
            out_shape=jax.ShapeDtypeStruct(held.shape, held.dtype),
            in_specs=[vmem, vmem, vmem],
            out_specs=pl.BlockSpec(memory_space=pl.ANY),
            scratch_shapes=[pltpu.VMEM((2, *held.shape[1:]), held.dtype), dma((2 * HALF + 3, CHUNKS))],
            compiler_params=pltpu.CompilerParams(vmem_limit_bytes=24 * 2**20),
        )(held, win, scaled)

    return jax.shard_map(
        step, mesh=mesh, in_specs=(P("vec", None), P("rep", None)),
        out_specs=P(None, "rep", "vec", None), check_vma=False,
    )
```

```python
import functools
import math

import jax
import jax.numpy as jnp
from jax import lax
from jax.experimental import pallas as pl
from jax.experimental.pallas import tpu as pltpu
from jax.sharding import PartitionSpec as P

HALF = 3
NEAR, OUTER, FAR = 0, 1, 2
AT = (3, 5, 2)
LAST = FAR
RELAY, ROUTED, WIDE = range(3)
LOW_END, LOW_MID, HIGH_MID, HIGH_END, RING = range(5)
ACROSS = (HIGH_END, HIGH_MID, LOW_MID, LOW_END)
BESIDE = (LOW_MID, LOW_END, HIGH_END, HIGH_MID)
MODES = (
    (ROUTED, WIDE, WIDE),
    (WIDE, WIDE, ROUTED),
    (ROUTED, WIDE, ROUTED),
    (ROUTED, WIDE, ROUTED),
    (RELAY, RELAY, RELAY),
)


def words(*parts):
    return " ".join(parts)


STEPS = (
    (
        words("up z00 z01 inward", "outward corner z10 z11", "z20 rows z21"),
        words("d00 d01 r0 d10", "d11 r1 h0"),
        words("h1"),
        words("d20 d21 r2"),
    ),
    (
        words("up z00 z10 z11", "z01 d00 rows d01", "corner r0 z20 z21", "r1 d10 d11"),
        words("h1"),
        words("h0"),
        words("d20 d21 r2"),
    ),
    (
        words("up inward z00 z10", "z11 z01 corner d00", "rows d01 z20 z21", "r1 d10 d11"),
        words("r0 h1"),
        words("h0"),
        words("d20 d21 r2"),
    ),
    (
        words("up z00 outward0 z01", "inward corner z10 outward1", "z11 z20 rows z21", "d00 d01"),
        words("r0 d10 d11 r1", "h0"),
        words("h1"),
        words("d20 d21 r2"),
    ),
    (
        words("z00 z10 z01 z11", "up d00 d01 corner", "rows z20 z21 d10", "d11 r0 d20 d21", "r1"),
        words("h0"),
        words("h1"),
        words("r2"),
    ),
)
CHUNKS = 1
SWAP = True
SIDES = (-1, 1)


def contract(left, right):
    return lax.dot_general(
        left, right, (((1,), (1,)), ((), ())), preferred_element_type=jnp.float32
    )


def inward(chip, chips):
    return 1 - 2 * (2 * chip // chips) if chips == 4 else 1 + 0 * chip


def pairs(i, core, way):
    if isinstance(i, int) and i == 3 and LAST == FAR:
        return 1, HALF + 1 - 2 * core, 2 * HALF * core
    if isinstance(i, int) and i == 3:
        return 5, HALF - 2 * way, HALF - 2 * way + 1 - 2 * core
    if LAST == FAR:
        step = way * (i % 2) - way * (i // 2)
        mine = HALF + 2 * step
        return (i > 0) + 2 * i, mine, mine + 1 - 2 * core
    near, far = i % 2, i // 2
    mine = HALF + 2 * way * near + far * (1 - 2 * core)
    other = (HALF + 2 * way * near + 1 - 2 * core) * (1 - far) + 2 * HALF * core * far
    return 3 * near + far, mine, other


def products(scaled, right, count):
    value = (contract(scaled, right) * (1.0 / math.sqrt(scaled.shape[1]))).astype(jnp.bfloat16)
    return value.reshape(count, scaled.shape[0] // count, right.shape[0])


def closing(n_vec, held, win, scaled, out_ref, last, sems):
    window, count, block_rows, fields = held.shape[0], held.shape[1], held.shape[2], win.shape[2]
    me = lax.axis_index("vec")
    base, first, second = pairs(3, me % 2, inward(me // 2, n_vec // 2))
    fresh = [second] if LAST == FAR else [first, second]

    def ready(i):
        return pltpu.make_async_copy(held.at[i], out_ref.at[i], sems.at[i, 0])

    some = count // CHUNKS

    def late(j, n):
        ks = pl.ds(n * some, some)
        return pltpu.make_async_copy(last.at[j, ks], out_ref.at[fresh[j], ks], sems.at[window + j, n])

    def others(action):
        for i in range(window):
            unlike = fresh[0] != i
            for spot in fresh[1:]:
                unlike = jnp.logical_and(unlike, spot != i)
            pl.when(unlike)(lambda i=i: action(i))

    with jax.named_scope("s"):
        others(lambda i: ready(i).start())
    right = win[base:base + 2].reshape(2 * block_rows, fields)
    for n in range(CHUNKS):
        with jax.named_scope(f"c{n}"):
            value = products(scaled[n * some * block_rows:(n + 1) * some * block_rows], right, some)
            for j in range(len(fresh)):
                h = 2 - len(fresh) + j
                last[j, n * some:(n + 1) * some] = value[:, :, h * block_rows:(h + 1) * block_rows]
                late(j, n).start()
    with jax.named_scope("w0"):
        others(lambda i: ready(i).wait())
    with jax.named_scope("w1"):
        for j in range(len(fresh)):
            for n in range(CHUNKS):
                late(j, n).wait()


def kernel(
    n_vec, n_a, n_b, vec_ref, index_ref, out_ref, win, scaled, wanted_ref, rows_ref, chip_ref, heard,
    out_sem, z_recv, f_recv, d_recv, r_recv, p_recv, h_recv, o_recv, local_sem, allow,
):
    block_rows, fields = vec_ref.shape
    count = index_ref.shape[1]
    n_rep = n_a * n_b
    chips = n_vec // 2
    part = block_rows // n_rep
    piece = part // 2
    me = lax.axis_index("vec")
    rep = lax.axis_index("rep")
    a, b = rep // n_b, rep % n_b
    chip, core = me // 2, me % 2
    partner = {"vec": me + 1 - 2 * core}
    way = inward(chip, chips)
    short = n_vec <= 16

    def chip_index(offset):
        return (chip + offset + chips) % chips

    def at_chip(offset, which):
        return {"vec": 2 * chip_index(offset) + which}

    def rep_of(da, db):
        return ((a + da + n_a) % n_a) * n_b + (b + db + n_b) % n_b

    direct = [(0, i) for i in range(1, n_b)] + [(i, 0) for i in range(1, n_a)]
    diagonal = [(i, j) for i in range(1, n_a) for j in range(1, n_b)]
    relays = {}
    for t, (da, db) in enumerate(direct):
        if da == 0:
            relays[t] = [((i, 0), diagonal.index((i, db))) for i in range(1, n_a)]
        else:
            relays[t] = [((0, j), diagonal.index((da, j))) for j in range(1, n_b)]
    side = [0 if da == 0 else 1 for da, _ in direct]

    own_copy = pltpu.make_async_copy(vec_ref, win.at[0], local_sem.at[0])
    index_copy = pltpu.make_async_copy(index_ref, wanted_ref, local_sem.at[1])
    own_copy.start()
    index_copy.start()

    def is_up(offset):
        return chip_index(offset) > chip

    def rep_is_up(da, db):
        return rep_of(da, db) > rep

    def number_of(flags):
        return sum((flag.astype(jnp.int32) for flag in flags), jnp.int32(0))

    def everywhere(action):
        def body(i, carry):
            action(i)
            return carry

        lax.fori_loop(1, chips, body, 0, unroll=short)

    barrier = pltpu.get_barrier_semaphore()
    lower = jnp.logical_not

    def meet(sem, when, device):
        pl.when(when)(lambda: pl.semaphore_signal(sem, inc=1, device_id=device))

    def allowed(i, times):
        pl.when(times > 0)(lambda: pl.semaphore_wait(allow.at[i], times))

    sides = (1, -1)
    everywhere(lambda i: meet(barrier, is_up(i), at_chip(i, core)))
    opposite = (1,) if chips == 4 else sides
    for step in opposite:
        meet(barrier, is_up(step), at_chip(step, 1 - core))
    for hop in direct:
        meet(barrier, rep_is_up(*hop), {"rep": rep_of(*hop)})
    pl.semaphore_signal(barrier, inc=1, device_id=partner)
    ups = number_of([is_up(step) for step in opposite])
    downs = number_of([chip > 0]) if chips == 4 else 2 - ups
    rep_ups = number_of([rep_is_up(*hop) for hop in direct])
    with jax.named_scope("barrier"):
        pl.semaphore_wait(barrier, chip + downs + (len(direct) - rep_ups) + 1)
    meet(allow.at[0], lower(is_up(-1)), at_chip(-1, core))
    everywhere(lambda i: meet(allow.at[1], lower(is_up(i)), at_chip(i, core)))
    for hop in direct:
        meet(allow.at[2], lower(rep_is_up(*hop)), {"rep": rep_of(*hop)})
    if chips == 4:
        meet(allow.at[2], chip > 0, at_chip(-1, 1 - core))
    else:
        for step in sides:
            meet(allow.at[2], lower(is_up(step)), at_chip(step, 1 - core))

    def remote(src, dst, send_sem, recv_sem, device):
        return pltpu.make_async_remote_copy(
            src_ref=src, dst_ref=dst, send_sem=send_sem, recv_sem=recv_sem, device_id=device
        )

    def arrive(rows, sem):
        spot = scaled.at[pl.ds(0, rows)]
        remote(spot, spot, out_sem.at[0], sem, partner).wait_recv()

    def gone(rows):
        spot = scaled.at[pl.ds(0, rows)]
        remote(spot, spot, out_sem.at[0], o_recv.at[0], partner).wait_send()

    def rows_at(which, h):
        return pl.ds(pl.multiple_of(which * part + h * piece, piece), piece)

    def quarter(da, db, h):
        return rows_at(rep_of(-da, -db), h)

    own = [rows_at(rep, h) for h in range(2)]

    if chips == 4:
        edge = jnp.logical_or(chip == 0, chip == chips - 1)
    else:
        edge = chip < 0

    def z_copy(step, which):
        looks = inward(chip_index(step), chips)
        slot = (1 + step * looks) // 2
        if which < 2:
            rows = own[which]
        else:
            rows = pl.ds(pl.multiple_of(rep_of(*diagonal[which - 2]) * part, part), part)
        return remote(
            vec_ref.at[rows], win.at[AT[NEAR] + (AT[OUTER] - AT[NEAR]) * slot, rows],
            out_sem.at[0], z_recv.at[slot, which] if which < 2 else r_recv.at[slot], at_chip(step, core),
        )

    def passes(slot):
        return lower(edge) if chips == 4 else core == slot

    def pass_on(slot, h):
        step = -way if slot == NEAR else way
        return remote(
            win.at[AT[slot], own[h]], win.at[AT[FAR], own[h]], out_sem.at[0], f_recv.at[h],
            at_chip(step, 1 - core),
        )

    def d_copy(slot, t, h):
        spot = win.at[AT[slot], own[h]]
        return remote(spot, spot, out_sem.at[0], d_recv.at[slot, h], {"rep": rep_of(*direct[t])})

    def routed_copy(slot, number, h):
        spot = win.at[AT[slot], own[h]]
        return remote(spot, spot, out_sem.at[0], r_recv.at[slot], {"rep": rep_of(*diagonal[number])})

    def r_copy(slot, t, hop):
        spot = win.at[AT[slot], quarter(*direct[t], side[t])]
        return remote(spot, spot, out_sem.at[0], r_recv.at[slot], {"rep": rep_of(*hop)})

    def hand(slot, rows):
        if slot != FAR:
            remote(
                win.at[AT[slot], rows], win.at[AT[slot] + 1, rows], out_sem.at[0], h_recv.at[slot], partner
            ).start()

    def handed(slot):
        arrive(block_rows, h_recv.at[slot])

    half = fields // 2

    def halves(src, dst, k, device):
        return remote(src, heard.at[dst], out_sem.at[1], p_recv.at[k], device)

    give_half = halves(rows_ref.at[1 - core], 0, 0, partner)
    swap = halves(chip_ref.at[1], chips, 2, partner)

    def rows_out(i):
        return halves(chip_ref.at[0], i, 1, at_chip(i, core))

    def first(slot, h, mode):
        arrive(piece, f_recv.at[h] if slot == FAR else z_recv.at[slot, h])
        if slot != FAR:
            pl.when(passes(slot))(lambda: pass_on(slot, h).start())
        if mode == ROUTED and slot != NEAR:
            for number in range(len(diagonal)):
                routed_copy(slot, number, h).start()
        for t in range(len(direct)):
            d_copy(slot, t, h).start()
        hand(slot, own[h])

    def second(slot, h, mode):
        if direct:
            arrive(len(direct) * piece, d_recv.at[slot, h])
        for t in range(len(direct)):
            if side[t] == h and mode == RELAY:
                for hop, number in relays[t]:
                    r_copy(slot, t, hop).start()
            hand(slot, quarter(*direct[t], h))

    def third(slot, mode, role):
        if diagonal:
            arrive(len(diagonal) * part, r_recv.at[slot])
        if slot == NEAR and widens(role):
            for spot in diagonal:
                rows = pl.ds(pl.multiple_of(rep_of(*spot) * part, part), part)
                remote(
                    win.at[AT[NEAR], rows], win.at[AT[FAR], rows], out_sem.at[0], r_recv.at[FAR],
                    at_chip(-way, 1 - core),
                ).start()
        for spot in diagonal:
            for h in range(2):
                hand(slot, quarter(*spot, h))

    partner_own = remote(vec_ref, win.at[1], out_sem.at[0], o_recv.at[0], partner)

    def prepare():
        mine, other = chip_ref[1].astype(jnp.float32), heard[chips].astype(jnp.float32)
        pivots = jnp.concatenate(
            [jnp.where(core == 0, mine, other), jnp.where(core == 0, other, mine)], axis=1
        )
        level = jnp.sum(pivots, axis=1, keepdims=True) / fields
        pivots = pivots - level
        block = win[0].astype(jnp.float32)
        for k in range(count):
            scaled[k * block_rows:(k + 1) * block_rows, :] = (block * pivots[k:k + 1, :]).astype(jnp.bfloat16)

    def compare(i):
        base, mine_at, other_at = pairs(i, core, way)
        value = products(scaled[...], win[pl.ds(base, 2)].reshape(2 * block_rows, fields), count)
        out_ref[mine_at] = value[:, :, :block_rows]
        out_ref[other_at] = value[:, :, block_rows:]

    def send_z(step, steps):
        for which in steps:
            z_copy(step, which).start()

    def send_wide(step):
        if diagonal:
            send_z(step, range(2, 2 + len(diagonal)))

    def extra(role):
        ends = role in (LOW_END, HIGH_END)
        inside = MODES[BESIDE[role]][OUTER] if ends else MODES[ACROSS[role]][NEAR]
        outside = MODES[ACROSS[role]][OUTER] if ends else MODES[BESIDE[role]][NEAR]
        return inside == WIDE, outside == WIDE

    def widens(role):
        return role in (LOW_MID, HIGH_MID) and MODES[BESIDE[role]][FAR] == WIDE

    def up():
        allowed(1, chips - 1 - chip)
        pl.when(is_up(-1))(lambda: send_z(-1, range(2)))
        everywhere(lambda i: pl.when(is_up(i))(lambda: rows_out(i).start()))

    def add_rows():
        spot = heard.at[pl.ds(1, chips - 1)]
        remote(spot, spot, out_sem.at[1], p_recv.at[1], partner).wait_recv()
        total = lax.fori_loop(
            1, chips, lambda i, total: total + heard[i].astype(jnp.float32),
            chip_ref[0].astype(jnp.float32), unroll=short,
        )
        chip_ref[1] = total.astype(jnp.bfloat16)
        swap.start()

    def run(steps, role):
        for name in steps.split():
            slot = int(name[1]) if name[1].isdigit() else None
            with jax.named_scope(name):
                if name == "up":
                    up()
                elif name in ("inward", "outward", "outward0", "outward1"):
                    if extra(role)[name != "inward"]:
                        for step in sides:
                            when = (way == step) == (name == "inward")
                            if name[-1].isdigit():
                                when = jnp.logical_and(when, core == int(name[-1]))
                            pl.when(when)(lambda: send_wide(step))
                elif name == "corner":
                    if direct:
                        pl.semaphore_wait(allow.at[3], len(direct))
                    if MODES[role][NEAR] == ROUTED:
                        for h in range(2):
                            for number in range(len(diagonal)):
                                routed_copy(NEAR, number, h).start()
                elif name == "rows":
                    add_rows()
                elif name[0] == "z":
                    first(slot, int(name[2]), MODES[role][slot])
                elif name[0] == "d":
                    second(slot, int(name[2]), MODES[role][slot])
                elif name[0] == "r":
                    third(slot, MODES[role][slot], role)
                else:
                    handed(slot)

    is_role = [chip == 0, chip == 1, chip == 2, chip == 3]

    def by_role(i):
        if chips != 4:
            run(STEPS[RING][i], RING)
            return
        for role in range(chips):
            pl.when(is_role[role])(lambda: run(STEPS[role][i], role))

    for h in range(2):
        for step in SIDES:
            pl.when(lower(is_up(step)))(lambda: z_copy(step, h).start())
    partner_own.start()

    index_copy.wait()
    own_copy.wait()
    wanted = wanted_ref[...] - me * block_rows
    spots = lax.broadcasted_iota(jnp.int32, (block_rows, count), 0)
    onehot = (spots == wanted).astype(jnp.bfloat16)
    mine = lax.dot_general(
        onehot, win[0], (((0,), (0,)), ((), ())), preferred_element_type=jnp.float32
    )
    rows_ref[0] = mine[:, :half].astype(jnp.bfloat16)
    rows_ref[1] = mine[:, half:].astype(jnp.bfloat16)
    give_half.start()
    with jax.named_scope("half"):
        give_half.wait_recv()
    both = rows_ref[core].astype(jnp.float32) + heard[0].astype(jnp.float32)
    chip_ref[0] = both.astype(jnp.bfloat16)
    everywhere(lambda i: pl.when(lower(is_up(i)))(lambda: rows_out(i).start()))

    @pl.when(is_up(1))
    def _():
        with jax.named_scope("next"):
            pl.semaphore_wait(allow.at[0], 1)
        send_z(1, range(2))

    with jax.named_scope("allow"):
        allowed(2, rep_ups + ups)
        for hop in direct:
            pl.semaphore_signal(allow.at[3], inc=1, device_id={"rep": rep_of(*hop)})
    def body(i, carry):
        for j in range(3):
            pl.when(i == j)(lambda: by_role(j))

        @pl.when(i == 0)
        def _():
            with jax.named_scope("pivots"):
                swap.wait_recv()
                arrive(block_rows, o_recv.at[0])
            with jax.named_scope("scaled"):
                prepare()

        with jax.named_scope("cmp"):
            compare(lax.select(jnp.logical_and(lower(edge), i > 0), 3 - i, i) if chips == 4 and SWAP else i)
        return carry

    lax.fori_loop(0, 3, body, 0)
    by_role(3)
    with jax.named_scope("drain"):
        relayed = sum(len(hops) for hops in relays.values()) * piece

        def total(role):
            rows = (3 if role == RING else 2) * part + 3 * block_rows + 3 * len(direct) * part
            for mode in MODES[role]:
                rows += relayed if mode == RELAY else len(diagonal) * part if mode == ROUTED else 0
            if role != RING:
                rows += (sum(extra(role)) + widens(role)) * len(diagonal) * part
            return rows + (2 * part if role in (LOW_MID, HIGH_MID) else 0)

        if chips != 4:
            gone(total(RING))
        else:
            for role in range(chips):
                pl.when(is_role[role])(lambda: gone(total(role)))
        spot = heard.at[pl.ds(0, chips + 1)]
        remote(spot, spot, out_sem.at[1], p_recv.at[1], partner).wait_send()


def solution(mesh):
    n_vec, n_rep = mesh.shape["vec"], mesh.shape["rep"]
    n_b = 2 if n_rep % 2 == 0 else 1
    n_a = n_rep // n_b
    assert n_vec % 2 == 0 and n_vec > 2 * HALF

    def step(vectors, pivot_index):
        rows, fields = vectors.shape
        count = pivot_index.shape[1]
        dma = pltpu.SemaphoreType.DMA
        vmem = pl.BlockSpec(memory_space=pltpu.VMEM)
        hbm = pl.BlockSpec(memory_space=pltpu.HBM)
        held, win, scaled = pl.pallas_call(
            functools.partial(kernel, n_vec, n_a, n_b),
            out_shape=(
                pltpu.VMEM((2 * HALF + 1, count, rows, rows), jnp.bfloat16),
                pltpu.VMEM((7, rows, fields), jnp.bfloat16),
                pltpu.VMEM((count * rows, fields), jnp.bfloat16),
            ),
            in_specs=[hbm, hbm],
            out_specs=(vmem, vmem, vmem),
            scratch_shapes=[
                pltpu.VMEM((1, count), jnp.int32),
                pltpu.VMEM((2, count, fields // 2), jnp.bfloat16),
                pltpu.VMEM((2, count, fields // 2), jnp.bfloat16),
                pltpu.VMEM((n_vec // 2 + 1, count, fields // 2), jnp.bfloat16),
                dma((2,)), dma((2, 2)), dma((2,)), dma((3, 2)), dma((3,)), dma((3,)), dma((2,)),
                dma((1,)), dma((2,)), pltpu.SemaphoreType.REGULAR((4,)),
            ],
            compiler_params=pltpu.CompilerParams(
                collective_id=0, has_side_effects=True, vmem_limit_bytes=60_800_000
            ),
        )(vectors, pivot_index)
        return pl.pallas_call(
            functools.partial(closing, n_vec),
            out_shape=jax.ShapeDtypeStruct(held.shape, held.dtype),
            in_specs=[vmem, vmem, vmem],
            out_specs=pl.BlockSpec(memory_space=pl.ANY),
            scratch_shapes=[pltpu.VMEM((2, *held.shape[1:]), held.dtype), dma((2 * HALF + 3, CHUNKS))],
            compiler_params=pltpu.CompilerParams(vmem_limit_bytes=24 * 2**20),
        )(held, win, scaled)

    return jax.shard_map(
        step, mesh=mesh, in_specs=(P("vec", None), P("rep", None)),
        out_specs=P(None, "rep", "vec", None), check_vma=False,
    )
```

```python
import functools
import math

import jax
import jax.numpy as jnp
from jax import lax
from jax.experimental import pallas as pl
from jax.experimental.pallas import tpu as pltpu
from jax.sharding import PartitionSpec as P

HALF = 3
NEAR, OUTER, FAR = 0, 1, 2
AT = (3, 5, 2)
LAST = FAR
RELAY, ROUTED, WIDE = range(3)
LOW_END, LOW_MID, HIGH_MID, HIGH_END, RING = range(5)
ACROSS = (HIGH_END, HIGH_MID, LOW_MID, LOW_END)
BESIDE = (LOW_MID, LOW_END, HIGH_END, HIGH_MID)
MODES = (
    (ROUTED, WIDE, WIDE),
    (WIDE, WIDE, ROUTED),
    (ROUTED, WIDE, ROUTED),
    (ROUTED, WIDE, ROUTED),
    (RELAY, RELAY, RELAY),
)


def words(*parts):
    return " ".join(parts)


STEPS = (
    (
        words("up z00 z01 inward", "outward corner z10 z11", "z20 rows z21 d00", "d01"),
        words("r0 d10 d11 r1", "h0"),
        words("h1"),
        words("d20 d21 r2"),
    ),
    (
        words("up z00 z10 z11", "z01 d00 rows d01", "corner r0 z20 z21", "r1 d10 d11"),
        words("h1"),
        words("h0"),
        words("d20 d21 r2"),
    ),
    (
        words("up inward z00 z10", "z11 z01 corner d00", "rows d01 z20 z21", "r1 d10 d11"),
        words("r0 h1"),
        words("h0"),
        words("d20 d21 r2"),
    ),
    (
        words("up z00 outward0 z01", "inward corner z10 outward1", "z11 z20 rows z21", "d00 d01"),
        words("r0 d10 d11 r1", "h0"),
        words("h1"),
        words("d20 d21 r2"),
    ),
    (
        words("z00 z10 z01 z11", "up d00 d01 corner", "rows z20 z21 d10", "d11 r0 d20 d21", "r1"),
        words("h0"),
        words("h1"),
        words("r2"),
    ),
)
CHUNKS = 1
SWAP = True
SIDES = (-1, 1)


def contract(left, right):
    return lax.dot_general(
        left, right, (((1,), (1,)), ((), ())), preferred_element_type=jnp.float32
    )


def inward(chip, chips):
    return 1 - 2 * (2 * chip // chips) if chips == 4 else 1 + 0 * chip


def pairs(i, core, way):
    if isinstance(i, int) and i == 3 and LAST == FAR:
        return 1, HALF + 1 - 2 * core, 2 * HALF * core
    if isinstance(i, int) and i == 3:
        return 5, HALF - 2 * way, HALF - 2 * way + 1 - 2 * core
    if LAST == FAR:
        step = way * (i % 2) - way * (i // 2)
        mine = HALF + 2 * step
        return (i > 0) + 2 * i, mine, mine + 1 - 2 * core
    near, far = i % 2, i // 2
    mine = HALF + 2 * way * near + far * (1 - 2 * core)
    other = (HALF + 2 * way * near + 1 - 2 * core) * (1 - far) + 2 * HALF * core * far
    return 3 * near + far, mine, other


def products(scaled, right, count):
    value = (contract(scaled, right) * (1.0 / math.sqrt(scaled.shape[1]))).astype(jnp.bfloat16)
    return value.reshape(count, scaled.shape[0] // count, right.shape[0])


def closing(n_vec, held, win, scaled, out_ref, last, sems):
    window, count, block_rows, fields = held.shape[0], held.shape[1], held.shape[2], win.shape[2]
    me = lax.axis_index("vec")
    base, first, second = pairs(3, me % 2, inward(me // 2, n_vec // 2))
    fresh = [second] if LAST == FAR else [first, second]

    def ready(i):
        return pltpu.make_async_copy(held.at[i], out_ref.at[i], sems.at[i, 0])

    some = count // CHUNKS

    def late(j, n):
        ks = pl.ds(n * some, some)
        return pltpu.make_async_copy(last.at[j, ks], out_ref.at[fresh[j], ks], sems.at[window + j, n])

    def others(action):
        for i in range(window):
            unlike = fresh[0] != i
            for spot in fresh[1:]:
                unlike = jnp.logical_and(unlike, spot != i)
            pl.when(unlike)(lambda i=i: action(i))

    with jax.named_scope("s"):
        others(lambda i: ready(i).start())
    right = win[base:base + 2].reshape(2 * block_rows, fields)
    for n in range(CHUNKS):
        with jax.named_scope(f"c{n}"):
            value = products(scaled[n * some * block_rows:(n + 1) * some * block_rows], right, some)
            for j in range(len(fresh)):
                h = 2 - len(fresh) + j
                last[j, n * some:(n + 1) * some] = value[:, :, h * block_rows:(h + 1) * block_rows]
                late(j, n).start()
    with jax.named_scope("w0"):
        others(lambda i: ready(i).wait())
    with jax.named_scope("w1"):
        for j in range(len(fresh)):
            for n in range(CHUNKS):
                late(j, n).wait()


def kernel(
    n_vec, n_a, n_b, vec_ref, index_ref, out_ref, win, scaled, wanted_ref, rows_ref, chip_ref, heard,
    out_sem, z_recv, f_recv, d_recv, r_recv, p_recv, h_recv, o_recv, local_sem, allow,
):
    block_rows, fields = vec_ref.shape
    count = index_ref.shape[1]
    n_rep = n_a * n_b
    chips = n_vec // 2
    part = block_rows // n_rep
    piece = part // 2
    me = lax.axis_index("vec")
    rep = lax.axis_index("rep")
    a, b = rep // n_b, rep % n_b
    chip, core = me // 2, me % 2
    partner = {"vec": me + 1 - 2 * core}
    way = inward(chip, chips)
    short = n_vec <= 16

    def chip_index(offset):
        return (chip + offset + chips) % chips

    def at_chip(offset, which):
        return {"vec": 2 * chip_index(offset) + which}

    def rep_of(da, db):
        return ((a + da + n_a) % n_a) * n_b + (b + db + n_b) % n_b

    direct = [(0, i) for i in range(1, n_b)] + [(i, 0) for i in range(1, n_a)]
    diagonal = [(i, j) for i in range(1, n_a) for j in range(1, n_b)]
    relays = {}
    for t, (da, db) in enumerate(direct):
        if da == 0:
            relays[t] = [((i, 0), diagonal.index((i, db))) for i in range(1, n_a)]
        else:
            relays[t] = [((0, j), diagonal.index((da, j))) for j in range(1, n_b)]
    side = [0 if da == 0 else 1 for da, _ in direct]

    own_copy = pltpu.make_async_copy(vec_ref, win.at[0], local_sem.at[0])
    index_copy = pltpu.make_async_copy(index_ref, wanted_ref, local_sem.at[1])
    own_copy.start()
    index_copy.start()

    def is_up(offset):
        return chip_index(offset) > chip

    def rep_is_up(da, db):
        return rep_of(da, db) > rep

    def number_of(flags):
        return sum((flag.astype(jnp.int32) for flag in flags), jnp.int32(0))

    def everywhere(action):
        def body(i, carry):
            action(i)
            return carry

        lax.fori_loop(1, chips, body, 0, unroll=short)

    barrier = pltpu.get_barrier_semaphore()
    lower = jnp.logical_not

    def meet(sem, when, device):
        pl.when(when)(lambda: pl.semaphore_signal(sem, inc=1, device_id=device))

    def allowed(i, times):
        pl.when(times > 0)(lambda: pl.semaphore_wait(allow.at[i], times))

    sides = (1, -1)
    everywhere(lambda i: meet(barrier, is_up(i), at_chip(i, core)))
    opposite = (1,) if chips == 4 else sides
    for step in opposite:
        meet(barrier, is_up(step), at_chip(step, 1 - core))
    for hop in direct:
        meet(barrier, rep_is_up(*hop), {"rep": rep_of(*hop)})
    pl.semaphore_signal(barrier, inc=1, device_id=partner)
    ups = number_of([is_up(step) for step in opposite])
    downs = number_of([chip > 0]) if chips == 4 else 2 - ups
    rep_ups = number_of([rep_is_up(*hop) for hop in direct])
    with jax.named_scope("barrier"):
        pl.semaphore_wait(barrier, chip + downs + (len(direct) - rep_ups) + 1)
    meet(allow.at[0], lower(is_up(-1)), at_chip(-1, core))
    everywhere(lambda i: meet(allow.at[1], lower(is_up(i)), at_chip(i, core)))
    for hop in direct:
        meet(allow.at[2], lower(rep_is_up(*hop)), {"rep": rep_of(*hop)})
    if chips == 4:
        meet(allow.at[2], chip > 0, at_chip(-1, 1 - core))
    else:
        for step in sides:
            meet(allow.at[2], lower(is_up(step)), at_chip(step, 1 - core))

    def remote(src, dst, send_sem, recv_sem, device):
        return pltpu.make_async_remote_copy(
            src_ref=src, dst_ref=dst, send_sem=send_sem, recv_sem=recv_sem, device_id=device
        )

    def arrive(rows, sem):
        spot = scaled.at[pl.ds(0, rows)]
        remote(spot, spot, out_sem.at[0], sem, partner).wait_recv()

    def gone(rows):
        spot = scaled.at[pl.ds(0, rows)]
        remote(spot, spot, out_sem.at[0], o_recv.at[0], partner).wait_send()

    def rows_at(which, h):
        return pl.ds(pl.multiple_of(which * part + h * piece, piece), piece)

    def quarter(da, db, h):
        return rows_at(rep_of(-da, -db), h)

    own = [rows_at(rep, h) for h in range(2)]

    if chips == 4:
        edge = jnp.logical_or(chip == 0, chip == chips - 1)
    else:
        edge = chip < 0

    def z_copy(step, which):
        looks = inward(chip_index(step), chips)
        slot = (1 + step * looks) // 2
        if which < 2:
            rows = own[which]
        else:
            rows = pl.ds(pl.multiple_of(rep_of(*diagonal[which - 2]) * part, part), part)
        return remote(
            vec_ref.at[rows], win.at[AT[NEAR] + (AT[OUTER] - AT[NEAR]) * slot, rows],
            out_sem.at[0], z_recv.at[slot, which] if which < 2 else r_recv.at[slot], at_chip(step, core),
        )

    def passes(slot):
        return lower(edge) if chips == 4 else core == slot

    def pass_on(slot, h):
        step = -way if slot == NEAR else way
        return remote(
            win.at[AT[slot], own[h]], win.at[AT[FAR], own[h]], out_sem.at[0], f_recv.at[h],
            at_chip(step, 1 - core),
        )

    def d_copy(slot, t, h):
        spot = win.at[AT[slot], own[h]]
        return remote(spot, spot, out_sem.at[0], d_recv.at[slot, h], {"rep": rep_of(*direct[t])})

    def routed_copy(slot, number, h):
        spot = win.at[AT[slot], own[h]]
        return remote(spot, spot, out_sem.at[0], r_recv.at[slot], {"rep": rep_of(*diagonal[number])})

    def r_copy(slot, t, hop):
        spot = win.at[AT[slot], quarter(*direct[t], side[t])]
        return remote(spot, spot, out_sem.at[0], r_recv.at[slot], {"rep": rep_of(*hop)})

    def hand(slot, rows):
        if slot != FAR:
            remote(
                win.at[AT[slot], rows], win.at[AT[slot] + 1, rows], out_sem.at[0], h_recv.at[slot], partner
            ).start()

    def handed(slot):
        arrive(block_rows, h_recv.at[slot])

    half = fields // 2

    def halves(src, dst, k, device):
        return remote(src, heard.at[dst], out_sem.at[1], p_recv.at[k], device)

    give_half = halves(rows_ref.at[1 - core], 0, 0, partner)
    swap = halves(chip_ref.at[1], chips, 2, partner)

    def rows_out(i):
        return halves(chip_ref.at[0], i, 1, at_chip(i, core))

    def first(slot, h, mode):
        arrive(piece, f_recv.at[h] if slot == FAR else z_recv.at[slot, h])
        if slot != FAR:
            pl.when(passes(slot))(lambda: pass_on(slot, h).start())
        if mode == ROUTED and slot != NEAR:
            for number in range(len(diagonal)):
                routed_copy(slot, number, h).start()
        for t in range(len(direct)):
            d_copy(slot, t, h).start()
        hand(slot, own[h])

    def second(slot, h, mode):
        if direct:
            arrive(len(direct) * piece, d_recv.at[slot, h])
        for t in range(len(direct)):
            if side[t] == h and mode == RELAY:
                for hop, number in relays[t]:
                    r_copy(slot, t, hop).start()
            hand(slot, quarter(*direct[t], h))

    def third(slot, mode, role):
        if diagonal:
            arrive(len(diagonal) * part, r_recv.at[slot])
        if slot == NEAR and widens(role):
            for spot in diagonal:
                rows = pl.ds(pl.multiple_of(rep_of(*spot) * part, part), part)
                remote(
                    win.at[AT[NEAR], rows], win.at[AT[FAR], rows], out_sem.at[0], r_recv.at[FAR],
                    at_chip(-way, 1 - core),
                ).start()
        for spot in diagonal:
            for h in range(2):
                hand(slot, quarter(*spot, h))

    partner_own = remote(vec_ref, win.at[1], out_sem.at[0], o_recv.at[0], partner)

    def prepare():
        mine, other = chip_ref[1].astype(jnp.float32), heard[chips].astype(jnp.float32)
        pivots = jnp.concatenate(
            [jnp.where(core == 0, mine, other), jnp.where(core == 0, other, mine)], axis=1
        )
        level = jnp.sum(pivots, axis=1, keepdims=True) / fields
        pivots = pivots - level
        block = win[0].astype(jnp.float32)
        for k in range(count):
            scaled[k * block_rows:(k + 1) * block_rows, :] = (block * pivots[k:k + 1, :]).astype(jnp.bfloat16)

    def compare(i):
        base, mine_at, other_at = pairs(i, core, way)
        value = products(scaled[...], win[pl.ds(base, 2)].reshape(2 * block_rows, fields), count)
        out_ref[mine_at] = value[:, :, :block_rows]
        out_ref[other_at] = value[:, :, block_rows:]

    def send_z(step, steps):
        for which in steps:
            z_copy(step, which).start()

    def send_wide(step):
        if diagonal:
            send_z(step, range(2, 2 + len(diagonal)))

    def extra(role):
        ends = role in (LOW_END, HIGH_END)
        inside = MODES[BESIDE[role]][OUTER] if ends else MODES[ACROSS[role]][NEAR]
        outside = MODES[ACROSS[role]][OUTER] if ends else MODES[BESIDE[role]][NEAR]
        return inside == WIDE, outside == WIDE

    def widens(role):
        return role in (LOW_MID, HIGH_MID) and MODES[BESIDE[role]][FAR] == WIDE

    def up():
        allowed(1, chips - 1 - chip)
        pl.when(is_up(-1))(lambda: send_z(-1, range(2)))
        everywhere(lambda i: pl.when(is_up(i))(lambda: rows_out(i).start()))

    def add_rows():
        spot = heard.at[pl.ds(1, chips - 1)]
        remote(spot, spot, out_sem.at[1], p_recv.at[1], partner).wait_recv()
        total = lax.fori_loop(
            1, chips, lambda i, total: total + heard[i].astype(jnp.float32),
            chip_ref[0].astype(jnp.float32), unroll=short,
        )
        chip_ref[1] = total.astype(jnp.bfloat16)
        swap.start()

    def run(steps, role):
        for name in steps.split():
            slot = int(name[1]) if name[1].isdigit() else None
            with jax.named_scope(name):
                if name == "up":
                    up()
                elif name in ("inward", "outward", "outward0", "outward1"):
                    if extra(role)[name != "inward"]:
                        for step in sides:
                            when = (way == step) == (name == "inward")
                            if name[-1].isdigit():
                                when = jnp.logical_and(when, core == int(name[-1]))
                            pl.when(when)(lambda: send_wide(step))
                elif name == "corner":
                    if direct:
                        pl.semaphore_wait(allow.at[3], len(direct))
                    if MODES[role][NEAR] == ROUTED:
                        for h in range(2):
                            for number in range(len(diagonal)):
                                routed_copy(NEAR, number, h).start()
                elif name == "rows":
                    add_rows()
                elif name[0] == "z":
                    first(slot, int(name[2]), MODES[role][slot])
                elif name[0] == "d":
                    second(slot, int(name[2]), MODES[role][slot])
                elif name[0] == "r":
                    third(slot, MODES[role][slot], role)
                else:
                    handed(slot)

    is_role = [chip == 0, chip == 1, chip == 2, chip == 3]

    def by_role(i):
        if chips != 4:
            run(STEPS[RING][i], RING)
            return
        for role in range(chips):
            pl.when(is_role[role])(lambda: run(STEPS[role][i], role))

    for h in range(2):
        for step in SIDES:
            pl.when(lower(is_up(step)))(lambda: z_copy(step, h).start())
    partner_own.start()

    index_copy.wait()
    own_copy.wait()
    wanted = wanted_ref[...] - me * block_rows
    spots = lax.broadcasted_iota(jnp.int32, (block_rows, count), 0)
    onehot = (spots == wanted).astype(jnp.bfloat16)
    mine = lax.dot_general(
        onehot, win[0], (((0,), (0,)), ((), ())), preferred_element_type=jnp.float32
    )
    rows_ref[0] = mine[:, :half].astype(jnp.bfloat16)
    rows_ref[1] = mine[:, half:].astype(jnp.bfloat16)
    give_half.start()
    with jax.named_scope("half"):
        give_half.wait_recv()
    both = rows_ref[core].astype(jnp.float32) + heard[0].astype(jnp.float32)
    chip_ref[0] = both.astype(jnp.bfloat16)
    everywhere(lambda i: pl.when(lower(is_up(i)))(lambda: rows_out(i).start()))

    @pl.when(is_up(1))
    def _():
        with jax.named_scope("next"):
            pl.semaphore_wait(allow.at[0], 1)
        send_z(1, range(2))

    with jax.named_scope("allow"):
        allowed(2, rep_ups + ups)
        for hop in direct:
            pl.semaphore_signal(allow.at[3], inc=1, device_id={"rep": rep_of(*hop)})
    def body(i, carry):
        for j in range(3):
            pl.when(i == j)(lambda: by_role(j))

        @pl.when(i == 0)
        def _():
            with jax.named_scope("pivots"):
                swap.wait_recv()
                arrive(block_rows, o_recv.at[0])
            with jax.named_scope("scaled"):
                prepare()

        with jax.named_scope("cmp"):
            compare(lax.select(jnp.logical_and(lower(edge), i > 0), 3 - i, i) if chips == 4 and SWAP else i)
        return carry

    lax.fori_loop(0, 3, body, 0)
    by_role(3)
    with jax.named_scope("drain"):
        relayed = sum(len(hops) for hops in relays.values()) * piece

        def total(role):
            rows = (3 if role == RING else 2) * part + 3 * block_rows + 3 * len(direct) * part
            for mode in MODES[role]:
                rows += relayed if mode == RELAY else len(diagonal) * part if mode == ROUTED else 0
            if role != RING:
                rows += (sum(extra(role)) + widens(role)) * len(diagonal) * part
            return rows + (2 * part if role in (LOW_MID, HIGH_MID) else 0)

        if chips != 4:
            gone(total(RING))
        else:
            for role in range(chips):
                pl.when(is_role[role])(lambda: gone(total(role)))
        spot = heard.at[pl.ds(0, chips + 1)]
        remote(spot, spot, out_sem.at[1], p_recv.at[1], partner).wait_send()


def solution(mesh):
    n_vec, n_rep = mesh.shape["vec"], mesh.shape["rep"]
    n_b = 2 if n_rep % 2 == 0 else 1
    n_a = n_rep // n_b
    assert n_vec % 2 == 0 and n_vec > 2 * HALF

    def step(vectors, pivot_index):
        rows, fields = vectors.shape
        count = pivot_index.shape[1]
        dma = pltpu.SemaphoreType.DMA
        vmem = pl.BlockSpec(memory_space=pltpu.VMEM)
        hbm = pl.BlockSpec(memory_space=pltpu.HBM)
        held, win, scaled = pl.pallas_call(
            functools.partial(kernel, n_vec, n_a, n_b),
            out_shape=(
                pltpu.VMEM((2 * HALF + 1, count, rows, rows), jnp.bfloat16),
                pltpu.VMEM((7, rows, fields), jnp.bfloat16),
                pltpu.VMEM((count * rows, fields), jnp.bfloat16),
            ),
            in_specs=[hbm, hbm],
            out_specs=(vmem, vmem, vmem),
            scratch_shapes=[
                pltpu.VMEM((1, count), jnp.int32),
                pltpu.VMEM((2, count, fields // 2), jnp.bfloat16),
                pltpu.VMEM((2, count, fields // 2), jnp.bfloat16),
                pltpu.VMEM((n_vec // 2 + 1, count, fields // 2), jnp.bfloat16),
                dma((2,)), dma((2, 2)), dma((2,)), dma((3, 2)), dma((3,)), dma((3,)), dma((2,)),
                dma((1,)), dma((2,)), pltpu.SemaphoreType.REGULAR((4,)),
            ],
            compiler_params=pltpu.CompilerParams(
                collective_id=0, has_side_effects=True, vmem_limit_bytes=60_800_000
            ),
        )(vectors, pivot_index)
        return pl.pallas_call(
            functools.partial(closing, n_vec),
            out_shape=jax.ShapeDtypeStruct(held.shape, held.dtype),
            in_specs=[vmem, vmem, vmem],
            out_specs=pl.BlockSpec(memory_space=pl.ANY),
            scratch_shapes=[pltpu.VMEM((2, *held.shape[1:]), held.dtype), dma((2 * HALF + 3, CHUNKS))],
            compiler_params=pltpu.CompilerParams(vmem_limit_bytes=24 * 2**20),
        )(held, win, scaled)

    return jax.shard_map(
        step, mesh=mesh, in_specs=(P("vec", None), P("rep", None)),
        out_specs=P(None, "rep", "vec", None), check_vma=False,
    )
```

```python
import functools
import math

import jax
import jax.numpy as jnp
from jax import lax
from jax.experimental import pallas as pl
from jax.experimental.pallas import tpu as pltpu
from jax.sharding import PartitionSpec as P

HALF = 3
NEAR, OUTER, FAR = 0, 1, 2
AT = (3, 5, 2)
LAST = FAR
RELAY, ROUTED, WIDE = range(3)
LOW_END, LOW_MID, HIGH_MID, HIGH_END, RING = range(5)
ACROSS = (HIGH_END, HIGH_MID, LOW_MID, LOW_END)
BESIDE = (LOW_MID, LOW_END, HIGH_END, HIGH_MID)
MODES = (
    (ROUTED, WIDE, WIDE),
    (WIDE, WIDE, ROUTED),
    (ROUTED, WIDE, ROUTED),
    (ROUTED, WIDE, ROUTED),
    (RELAY, RELAY, RELAY),
)


def words(*parts):
    return " ".join(parts)


STEPS = (
    (
        words("up z00 z01 inward", "outward corner z10 z11", "rows z20 z21 d00", "d01"),
        words("r0 d10 d11 r1", "h0"),
        words("h1"),
        words("d20 d21 r2"),
    ),
    (
        words("up z00 z10 z11", "z01 d00 rows d01", "corner r0 z20 z21", "r1 d10 d11"),
        words("h1"),
        words("h0"),
        words("d20 d21 r2"),
    ),
    (
        words("up inward z00 z10", "z11 z01 corner d00", "rows d01 z20 z21", "r1 d10 d11"),
        words("r0 h1"),
        words("h0"),
        words("d20 d21 r2"),
    ),
    (
        words("up z00 outward0 z01", "inward corner z10 outward1", "z11 z20 rows z21", "d00 d01"),
        words("r0 d10 d11 r1", "h0"),
        words("h1"),
        words("d20 d21 r2"),
    ),
    (
        words("z00 z10 z01 z11", "up d00 d01 corner", "rows z20 z21 d10", "d11 r0 d20 d21", "r1"),
        words("h0"),
        words("h1"),
        words("r2"),
    ),
)
CHUNKS = 1
SWAP = True
SIDES = (-1, 1)


def contract(left, right):
    return lax.dot_general(
        left, right, (((1,), (1,)), ((), ())), preferred_element_type=jnp.float32
    )


def inward(chip, chips):
    return 1 - 2 * (2 * chip // chips) if chips == 4 else 1 + 0 * chip


def pairs(i, core, way):
    if isinstance(i, int) and i == 3 and LAST == FAR:
        return 1, HALF + 1 - 2 * core, 2 * HALF * core
    if isinstance(i, int) and i == 3:
        return 5, HALF - 2 * way, HALF - 2 * way + 1 - 2 * core
    if LAST == FAR:
        step = way * (i % 2) - way * (i // 2)
        mine = HALF + 2 * step
        return (i > 0) + 2 * i, mine, mine + 1 - 2 * core
    near, far = i % 2, i // 2
    mine = HALF + 2 * way * near + far * (1 - 2 * core)
    other = (HALF + 2 * way * near + 1 - 2 * core) * (1 - far) + 2 * HALF * core * far
    return 3 * near + far, mine, other


def products(scaled, right, count):
    value = (contract(scaled, right) * (1.0 / math.sqrt(scaled.shape[1]))).astype(jnp.bfloat16)
    return value.reshape(count, scaled.shape[0] // count, right.shape[0])


def closing(n_vec, held, win, scaled, out_ref, last, sems):
    window, count, block_rows, fields = held.shape[0], held.shape[1], held.shape[2], win.shape[2]
    me = lax.axis_index("vec")
    base, first, second = pairs(3, me % 2, inward(me // 2, n_vec // 2))
    fresh = [second] if LAST == FAR else [first, second]

    def ready(i):
        return pltpu.make_async_copy(held.at[i], out_ref.at[i], sems.at[i, 0])

    some = count // CHUNKS

    def late(j, n):
        ks = pl.ds(n * some, some)
        return pltpu.make_async_copy(last.at[j, ks], out_ref.at[fresh[j], ks], sems.at[window + j, n])

    def others(action):
        for i in range(window):
            unlike = fresh[0] != i
            for spot in fresh[1:]:
                unlike = jnp.logical_and(unlike, spot != i)
            pl.when(unlike)(lambda i=i: action(i))

    with jax.named_scope("s"):
        others(lambda i: ready(i).start())
    right = win[base:base + 2].reshape(2 * block_rows, fields)
    for n in range(CHUNKS):
        with jax.named_scope(f"c{n}"):
            value = products(scaled[n * some * block_rows:(n + 1) * some * block_rows], right, some)
            for j in range(len(fresh)):
                h = 2 - len(fresh) + j
                last[j, n * some:(n + 1) * some] = value[:, :, h * block_rows:(h + 1) * block_rows]
                late(j, n).start()
    with jax.named_scope("w0"):
        others(lambda i: ready(i).wait())
    with jax.named_scope("w1"):
        for j in range(len(fresh)):
            for n in range(CHUNKS):
                late(j, n).wait()


def kernel(
    n_vec, n_a, n_b, vec_ref, index_ref, out_ref, win, scaled, wanted_ref, rows_ref, chip_ref, heard,
    out_sem, z_recv, f_recv, d_recv, r_recv, p_recv, h_recv, o_recv, local_sem, allow,
):
    block_rows, fields = vec_ref.shape
    count = index_ref.shape[1]
    n_rep = n_a * n_b
    chips = n_vec // 2
    part = block_rows // n_rep
    piece = part // 2
    me = lax.axis_index("vec")
    rep = lax.axis_index("rep")
    a, b = rep // n_b, rep % n_b
    chip, core = me // 2, me % 2
    partner = {"vec": me + 1 - 2 * core}
    way = inward(chip, chips)
    short = n_vec <= 16

    def chip_index(offset):
        return (chip + offset + chips) % chips

    def at_chip(offset, which):
        return {"vec": 2 * chip_index(offset) + which}

    def rep_of(da, db):
        return ((a + da + n_a) % n_a) * n_b + (b + db + n_b) % n_b

    direct = [(0, i) for i in range(1, n_b)] + [(i, 0) for i in range(1, n_a)]
    diagonal = [(i, j) for i in range(1, n_a) for j in range(1, n_b)]
    relays = {}
    for t, (da, db) in enumerate(direct):
        if da == 0:
            relays[t] = [((i, 0), diagonal.index((i, db))) for i in range(1, n_a)]
        else:
            relays[t] = [((0, j), diagonal.index((da, j))) for j in range(1, n_b)]
    side = [0 if da == 0 else 1 for da, _ in direct]

    own_copy = pltpu.make_async_copy(vec_ref, win.at[0], local_sem.at[0])
    index_copy = pltpu.make_async_copy(index_ref, wanted_ref, local_sem.at[1])
    own_copy.start()
    index_copy.start()

    def is_up(offset):
        return chip_index(offset) > chip

    def rep_is_up(da, db):
        return rep_of(da, db) > rep

    def number_of(flags):
        return sum((flag.astype(jnp.int32) for flag in flags), jnp.int32(0))

    def everywhere(action):
        def body(i, carry):
            action(i)
            return carry

        lax.fori_loop(1, chips, body, 0, unroll=short)

    barrier = pltpu.get_barrier_semaphore()
    lower = jnp.logical_not

    def meet(sem, when, device):
        pl.when(when)(lambda: pl.semaphore_signal(sem, inc=1, device_id=device))

    def allowed(i, times):
        pl.when(times > 0)(lambda: pl.semaphore_wait(allow.at[i], times))

    sides = (1, -1)
    everywhere(lambda i: meet(barrier, is_up(i), at_chip(i, core)))
    opposite = (1,) if chips == 4 else sides
    for step in opposite:
        meet(barrier, is_up(step), at_chip(step, 1 - core))
    for hop in direct:
        meet(barrier, rep_is_up(*hop), {"rep": rep_of(*hop)})
    pl.semaphore_signal(barrier, inc=1, device_id=partner)
    ups = number_of([is_up(step) for step in opposite])
    downs = number_of([chip > 0]) if chips == 4 else 2 - ups
    rep_ups = number_of([rep_is_up(*hop) for hop in direct])
    with jax.named_scope("barrier"):
        pl.semaphore_wait(barrier, chip + downs + (len(direct) - rep_ups) + 1)
    meet(allow.at[0], lower(is_up(-1)), at_chip(-1, core))
    everywhere(lambda i: meet(allow.at[1], lower(is_up(i)), at_chip(i, core)))
    for hop in direct:
        meet(allow.at[2], lower(rep_is_up(*hop)), {"rep": rep_of(*hop)})
    if chips == 4:
        meet(allow.at[2], chip > 0, at_chip(-1, 1 - core))
    else:
        for step in sides:
            meet(allow.at[2], lower(is_up(step)), at_chip(step, 1 - core))

    def remote(src, dst, send_sem, recv_sem, device):
        return pltpu.make_async_remote_copy(
            src_ref=src, dst_ref=dst, send_sem=send_sem, recv_sem=recv_sem, device_id=device
        )

    def arrive(rows, sem):
        spot = scaled.at[pl.ds(0, rows)]
        remote(spot, spot, out_sem.at[0], sem, partner).wait_recv()

    def gone(rows):
        spot = scaled.at[pl.ds(0, rows)]
        remote(spot, spot, out_sem.at[0], o_recv.at[0], partner).wait_send()

    def rows_at(which, h):
        return pl.ds(pl.multiple_of(which * part + h * piece, piece), piece)

    def quarter(da, db, h):
        return rows_at(rep_of(-da, -db), h)

    own = [rows_at(rep, h) for h in range(2)]

    if chips == 4:
        edge = jnp.logical_or(chip == 0, chip == chips - 1)
    else:
        edge = chip < 0

    def z_copy(step, which):
        looks = inward(chip_index(step), chips)
        slot = (1 + step * looks) // 2
        if which < 2:
            rows = own[which]
        else:
            rows = pl.ds(pl.multiple_of(rep_of(*diagonal[which - 2]) * part, part), part)
        return remote(
            vec_ref.at[rows], win.at[AT[NEAR] + (AT[OUTER] - AT[NEAR]) * slot, rows],
            out_sem.at[0], z_recv.at[slot, which] if which < 2 else r_recv.at[slot], at_chip(step, core),
        )

    def passes(slot):
        return lower(edge) if chips == 4 else core == slot

    def pass_on(slot, h):
        step = -way if slot == NEAR else way
        return remote(
            win.at[AT[slot], own[h]], win.at[AT[FAR], own[h]], out_sem.at[0], f_recv.at[h],
            at_chip(step, 1 - core),
        )

    def d_copy(slot, t, h):
        spot = win.at[AT[slot], own[h]]
        return remote(spot, spot, out_sem.at[0], d_recv.at[slot, h], {"rep": rep_of(*direct[t])})

    def routed_copy(slot, number, h):
        spot = win.at[AT[slot], own[h]]
        return remote(spot, spot, out_sem.at[0], r_recv.at[slot], {"rep": rep_of(*diagonal[number])})

    def r_copy(slot, t, hop):
        spot = win.at[AT[slot], quarter(*direct[t], side[t])]
        return remote(spot, spot, out_sem.at[0], r_recv.at[slot], {"rep": rep_of(*hop)})

    def hand(slot, rows):
        if slot != FAR:
            remote(
                win.at[AT[slot], rows], win.at[AT[slot] + 1, rows], out_sem.at[0], h_recv.at[slot], partner
            ).start()

    def handed(slot):
        arrive(block_rows, h_recv.at[slot])

    half = fields // 2

    def halves(src, dst, k, device):
        return remote(src, heard.at[dst], out_sem.at[1], p_recv.at[k], device)

    give_half = halves(rows_ref.at[1 - core], 0, 0, partner)
    swap = halves(chip_ref.at[1], chips, 2, partner)

    def rows_out(i):
        return halves(chip_ref.at[0], i, 1, at_chip(i, core))

    def first(slot, h, mode):
        arrive(piece, f_recv.at[h] if slot == FAR else z_recv.at[slot, h])
        if slot != FAR:
            pl.when(passes(slot))(lambda: pass_on(slot, h).start())
        if mode == ROUTED and slot != NEAR:
            for number in range(len(diagonal)):
                routed_copy(slot, number, h).start()
        for t in range(len(direct)):
            d_copy(slot, t, h).start()
        hand(slot, own[h])

    def second(slot, h, mode):
        if direct:
            arrive(len(direct) * piece, d_recv.at[slot, h])
        for t in range(len(direct)):
            if side[t] == h and mode == RELAY:
                for hop, number in relays[t]:
                    r_copy(slot, t, hop).start()
            hand(slot, quarter(*direct[t], h))

    def third(slot, mode, role):
        if diagonal:
            arrive(len(diagonal) * part, r_recv.at[slot])
        if slot == NEAR and widens(role):
            for spot in diagonal:
                rows = pl.ds(pl.multiple_of(rep_of(*spot) * part, part), part)
                remote(
                    win.at[AT[NEAR], rows], win.at[AT[FAR], rows], out_sem.at[0], r_recv.at[FAR],
                    at_chip(-way, 1 - core),
                ).start()
        for spot in diagonal:
            for h in range(2):
                hand(slot, quarter(*spot, h))

    partner_own = remote(vec_ref, win.at[1], out_sem.at[0], o_recv.at[0], partner)

    def prepare():
        mine, other = chip_ref[1].astype(jnp.float32), heard[chips].astype(jnp.float32)
        pivots = jnp.concatenate(
            [jnp.where(core == 0, mine, other), jnp.where(core == 0, other, mine)], axis=1
        )
        level = jnp.sum(pivots, axis=1, keepdims=True) / fields
        pivots = pivots - level
        block = win[0].astype(jnp.float32)
        for k in range(count):
            scaled[k * block_rows:(k + 1) * block_rows, :] = (block * pivots[k:k + 1, :]).astype(jnp.bfloat16)

    def compare(i):
        base, mine_at, other_at = pairs(i, core, way)
        value = products(scaled[...], win[pl.ds(base, 2)].reshape(2 * block_rows, fields), count)
        out_ref[mine_at] = value[:, :, :block_rows]
        out_ref[other_at] = value[:, :, block_rows:]

    def send_z(step, steps):
        for which in steps:
            z_copy(step, which).start()

    def send_wide(step):
        if diagonal:
            send_z(step, range(2, 2 + len(diagonal)))

    def extra(role):
        ends = role in (LOW_END, HIGH_END)
        inside = MODES[BESIDE[role]][OUTER] if ends else MODES[ACROSS[role]][NEAR]
        outside = MODES[ACROSS[role]][OUTER] if ends else MODES[BESIDE[role]][NEAR]
        return inside == WIDE, outside == WIDE

    def widens(role):
        return role in (LOW_MID, HIGH_MID) and MODES[BESIDE[role]][FAR] == WIDE

    def up():
        allowed(1, chips - 1 - chip)
        pl.when(is_up(-1))(lambda: send_z(-1, range(2)))
        everywhere(lambda i: pl.when(is_up(i))(lambda: rows_out(i).start()))

    def add_rows():
        spot = heard.at[pl.ds(1, chips - 1)]
        remote(spot, spot, out_sem.at[1], p_recv.at[1], partner).wait_recv()
        total = lax.fori_loop(
            1, chips, lambda i, total: total + heard[i].astype(jnp.float32),
            chip_ref[0].astype(jnp.float32), unroll=short,
        )
        chip_ref[1] = total.astype(jnp.bfloat16)
        swap.start()

    def run(steps, role):
        for name in steps.split():
            slot = int(name[1]) if name[1].isdigit() else None
            with jax.named_scope(name):
                if name == "up":
                    up()
                elif name in ("inward", "outward", "outward0", "outward1"):
                    if extra(role)[name != "inward"]:
                        for step in sides:
                            when = (way == step) == (name == "inward")
                            if name[-1].isdigit():
                                when = jnp.logical_and(when, core == int(name[-1]))
                            pl.when(when)(lambda: send_wide(step))
                elif name == "corner":
                    if direct:
                        pl.semaphore_wait(allow.at[3], len(direct))
                    if MODES[role][NEAR] == ROUTED:
                        for h in range(2):
                            for number in range(len(diagonal)):
                                routed_copy(NEAR, number, h).start()
                elif name == "rows":
                    add_rows()
                elif name[0] == "z":
                    first(slot, int(name[2]), MODES[role][slot])
                elif name[0] == "d":
                    second(slot, int(name[2]), MODES[role][slot])
                elif name[0] == "r":
                    third(slot, MODES[role][slot], role)
                else:
                    handed(slot)

    is_role = [chip == 0, chip == 1, chip == 2, chip == 3]

    def by_role(i):
        if chips != 4:
            run(STEPS[RING][i], RING)
            return
        for role in range(chips):
            pl.when(is_role[role])(lambda: run(STEPS[role][i], role))

    for h in range(2):
        for step in SIDES:
            pl.when(lower(is_up(step)))(lambda: z_copy(step, h).start())
    partner_own.start()

    index_copy.wait()
    own_copy.wait()
    wanted = wanted_ref[...] - me * block_rows
    spots = lax.broadcasted_iota(jnp.int32, (block_rows, count), 0)
    onehot = (spots == wanted).astype(jnp.bfloat16)
    mine = lax.dot_general(
        onehot, win[0], (((0,), (0,)), ((), ())), preferred_element_type=jnp.float32
    )
    rows_ref[0] = mine[:, :half].astype(jnp.bfloat16)
    rows_ref[1] = mine[:, half:].astype(jnp.bfloat16)
    give_half.start()
    with jax.named_scope("half"):
        give_half.wait_recv()
    both = rows_ref[core].astype(jnp.float32) + heard[0].astype(jnp.float32)
    chip_ref[0] = both.astype(jnp.bfloat16)
    everywhere(lambda i: pl.when(lower(is_up(i)))(lambda: rows_out(i).start()))

    @pl.when(is_up(1))
    def _():
        with jax.named_scope("next"):
            pl.semaphore_wait(allow.at[0], 1)
        send_z(1, range(2))

    with jax.named_scope("allow"):
        allowed(2, rep_ups + ups)
        for hop in direct:
            pl.semaphore_signal(allow.at[3], inc=1, device_id={"rep": rep_of(*hop)})
    def body(i, carry):
        for j in range(3):
            pl.when(i == j)(lambda: by_role(j))

        @pl.when(i == 0)
        def _():
            with jax.named_scope("pivots"):
                swap.wait_recv()
                arrive(block_rows, o_recv.at[0])
            with jax.named_scope("scaled"):
                prepare()

        with jax.named_scope("cmp"):
            compare(lax.select(jnp.logical_and(lower(edge), i > 0), 3 - i, i) if chips == 4 and SWAP else i)
        return carry

    lax.fori_loop(0, 3, body, 0)
    by_role(3)
    with jax.named_scope("drain"):
        relayed = sum(len(hops) for hops in relays.values()) * piece

        def total(role):
            rows = (3 if role == RING else 2) * part + 3 * block_rows + 3 * len(direct) * part
            for mode in MODES[role]:
                rows += relayed if mode == RELAY else len(diagonal) * part if mode == ROUTED else 0
            if role != RING:
                rows += (sum(extra(role)) + widens(role)) * len(diagonal) * part
            return rows + (2 * part if role in (LOW_MID, HIGH_MID) else 0)

        if chips != 4:
            gone(total(RING))
        else:
            for role in range(chips):
                pl.when(is_role[role])(lambda: gone(total(role)))
        spot = heard.at[pl.ds(0, chips + 1)]
        remote(spot, spot, out_sem.at[1], p_recv.at[1], partner).wait_send()


def solution(mesh):
    n_vec, n_rep = mesh.shape["vec"], mesh.shape["rep"]
    n_b = 2 if n_rep % 2 == 0 else 1
    n_a = n_rep // n_b
    assert n_vec % 2 == 0 and n_vec > 2 * HALF

    def step(vectors, pivot_index):
        rows, fields = vectors.shape
        count = pivot_index.shape[1]
        dma = pltpu.SemaphoreType.DMA
        vmem = pl.BlockSpec(memory_space=pltpu.VMEM)
        hbm = pl.BlockSpec(memory_space=pltpu.HBM)
        held, win, scaled = pl.pallas_call(
            functools.partial(kernel, n_vec, n_a, n_b),
            out_shape=(
                pltpu.VMEM((2 * HALF + 1, count, rows, rows), jnp.bfloat16),
                pltpu.VMEM((7, rows, fields), jnp.bfloat16),
                pltpu.VMEM((count * rows, fields), jnp.bfloat16),
            ),
            in_specs=[hbm, hbm],
            out_specs=(vmem, vmem, vmem),
            scratch_shapes=[
                pltpu.VMEM((1, count), jnp.int32),
                pltpu.VMEM((2, count, fields // 2), jnp.bfloat16),
                pltpu.VMEM((2, count, fields // 2), jnp.bfloat16),
                pltpu.VMEM((n_vec // 2 + 1, count, fields // 2), jnp.bfloat16),
                dma((2,)), dma((2, 2)), dma((2,)), dma((3, 2)), dma((3,)), dma((3,)), dma((2,)),
                dma((1,)), dma((2,)), pltpu.SemaphoreType.REGULAR((4,)),
            ],
            compiler_params=pltpu.CompilerParams(
                collective_id=0, has_side_effects=True, vmem_limit_bytes=60_800_000
            ),
        )(vectors, pivot_index)
        return pl.pallas_call(
            functools.partial(closing, n_vec),
            out_shape=jax.ShapeDtypeStruct(held.shape, held.dtype),
            in_specs=[vmem, vmem, vmem],
            out_specs=pl.BlockSpec(memory_space=pl.ANY),
            scratch_shapes=[pltpu.VMEM((2, *held.shape[1:]), held.dtype), dma((2 * HALF + 3, CHUNKS))],
            compiler_params=pltpu.CompilerParams(vmem_limit_bytes=24 * 2**20),
        )(held, win, scaled)

    return jax.shard_map(
        step, mesh=mesh, in_specs=(P("vec", None), P("rep", None)),
        out_specs=P(None, "rep", "vec", None), check_vma=False,
    )
```
